128 devices in a mesh: tile: 32 (over y, x, core), sub: 4 (over z).
Axes of the slice: x: 4, y: 4, z: 4, core: 2. Of those that a mesh axis runs over, the one named last changes fastest.
Arguments:
- right_side: float32 [8, 524288], P(None, ('tile', 'sub')), may hold values from -6 to 6
- point_order: int32 [128, 4096], P(('tile', 'sub')), may hold values from 0 to 4095, each once within a row
- noise_var: float32 [524288], P(('tile', 'sub')), may hold values from 0.1 to 1
- block_pairs: int32 [12288, 2], P(('tile', 'sub')), may hold values from -1 to 2047, as said below
- pair_blocks: bfloat16 [12288, 256, 256], P(('tile', 'sub')), as said below
- diag_blocks: bfloat16 [2048, 256, 256], P(('tile', 'sub')), as said below
Outputs:
- solution: float32 [8, 524288], P(None, ('tile', 'sub'))
- residual: float32 [8, 524288], P(None, ('tile', 'sub'))
The draws below stay inside these ranges and needn't reach their ends.
Inputs may be any that keep to these rules, and one draw needn't show every extreme that they name: `block_pairs`: the blocks form a grid of rows of 16 blocks in row-major order; device d (tile slowest, then sub) owns blocks 16 d to 16 d + 15, one grid row. A slot holds (r, c) with c the right, lower-left, lower or lower-right grid neighbour of r, or (-1, -1) when empty; every such neighbouring pair is held exactly once, by a device of the tile that owns r. On each device the live slots come first, and in every tile some device has all 96 slots live. pair_blocks[p] has the rows of block r and the columns of block c of block_pairs[p], and is zero for an empty slot; with diag_blocks these are the bfloat16 values of all nonzero blocks of a kernel matrix that is positive semi-definite before rounding. Each diag_blocks[q] is symmetric.
All inputs are finite; a program needn't handle non-finite values.
Results may differ from the reference program's by a relative error of at most 0.0075.
Values may be sent and summed in bfloat16 or wider, within the bound.
A program may use at most 64 MiB of HBM per device.

```python
import math
import jax
import jax.numpy as jnp
from jax import lax

RHS = 8
BLOCK = 256
BLK_DEV = 16
ITERS = 3
PAIR_DEV = 96
GRID_W = 16
BLOCKS = 2048
POINTS = 524288
PTS_DEV = 4096
N_SUB = 4
DEVICES = 128


AMPLITUDE = 0.0625


def point_coords(key):
    spread = jax.random.uniform(key, (BLOCKS, BLOCK, 2), jnp.float32)
    block_ids = jnp.arange(BLOCKS, dtype=jnp.int32)
    across = (block_ids % GRID_W).astype(jnp.float32)[:, None]
    downward = (block_ids // GRID_W).astype(jnp.float32)[:, None]
    return (spread[:, :, 0] + across, spread[:, :, 1] + downward)


def wendland(first_x, first_y, second_x, second_y):
    delta_x = first_x[:, None] - second_x[None, :]
    delta_y = first_y[:, None] - second_y[None, :]
    radius = jnp.sqrt(delta_x * delta_x + delta_y * delta_y)
    inside = jnp.maximum(1.0 - radius, 0.0)
    return AMPLITUDE * inside * inside * inside * inside * (4.0 * radius + 1.0)


def pair_table(key):
    tile_count = DEVICES // N_SUB
    tile_blocks = N_SUB * BLK_DEV
    slot_count = 4 * tile_blocks
    slot_ids = jnp.arange(slot_count, dtype=jnp.int32)
    kind_ids = slot_ids % 4
    row_block = jnp.arange(tile_count, dtype=jnp.int32)[:, None] * tile_blocks + (slot_ids // 4)[None, :]
    grid_row = row_block // GRID_W
    grid_col = row_block % GRID_W
    step_row = jnp.where(kind_ids == 0, 0, 1)[None, :]
    step_col = jnp.where(kind_ids == 0, 1, kind_ids - 2)[None, :]
    other_row = grid_row + step_row
    other_col = grid_col + step_col
    is_valid = (other_col >= 0) & (other_col < GRID_W) & (other_row < BLOCKS // GRID_W)
    partner = other_row * GRID_W + other_col
    score_key, rotation_key = jax.random.split(key)
    scores = jax.random.randint(score_key, (tile_count, slot_count), 0, 1 << 18)
    sort_keys = jnp.where(is_valid, scores * slot_count + slot_ids[None, :], (1 << 29) + slot_ids[None, :])
    ranked = jnp.argsort(sort_keys, axis=1).astype(jnp.int32)
    live_count = jnp.sum(is_valid.astype(jnp.int32), axis=1)
    capacity = jnp.array([12, 8, 7, 5], jnp.int32) * BLK_DEV // 2
    offsets = jnp.array([0, 12, 20, 27], jnp.int32) * BLK_DEV // 2
    rotation = jax.random.randint(rotation_key, (tile_count, 1), 0, 4)
    position = (jnp.arange(N_SUB, dtype=jnp.int32)[None, :] + rotation) % 4
    held_cap = capacity[position]
    held_start = offsets[position]
    slot_pos = jnp.arange(PAIR_DEV, dtype=jnp.int32)
    deal_index = held_start[:, :, None] + slot_pos[None, None, :]
    is_used = (slot_pos[None, None, :] < held_cap[:, :, None]) & (deal_index < live_count[:, None, None])
    picked = jnp.take_along_axis(ranked, jnp.minimum(deal_index, slot_count - 1).reshape(tile_count, -1), axis=1)
    row_ids = jnp.take_along_axis(row_block, picked, axis=1).reshape(tile_count, N_SUB, PAIR_DEV)
    col_ids = jnp.take_along_axis(partner, picked, axis=1).reshape(tile_count, N_SUB, PAIR_DEV)
    row_ids = jnp.where(is_used, row_ids, -1)
    col_ids = jnp.where(is_used, col_ids, -1)
    return jnp.stack([row_ids, col_ids], axis=-1).reshape(DEVICES * PAIR_DEV, 2).astype(jnp.int32)


def draw_block_pairs(key, part):
    return pair_table(jax.random.fold_in(key, 3))


def draw_pair_blocks(key, part):
    table = pair_table(jax.random.fold_in(key, 3))
    across, downward = point_coords(jax.random.fold_in(key, 5))
    live_flag = (table[:, 0] >= 0).astype(jnp.float32)
    first_id = jnp.maximum(table[:, 0], 0)
    second = jnp.maximum(table[:, 1], 0)

    def one_block(entry_data):
        row_id, col_id, flag_value = entry_data
        values = wendland(across[row_id], downward[row_id], across[col_id], downward[col_id])
        return (values * flag_value).astype(jnp.bfloat16)
    return lax.map(one_block, (first_id, second, live_flag))


def draw_diag_blocks(key, part):
    across, downward = point_coords(jax.random.fold_in(key, 5))

    def one_block(entry_data):
        block_x, block_y = entry_data
        return wendland(block_x, block_y, block_x, block_y).astype(jnp.bfloat16)
    return lax.map(one_block, (across, downward))


def block_scale(stream_key, shape, cuts, smallest, high):
    loudness = 1.0
    for axis_at, shards_of in cuts:
        heights = jax.random.uniform(jax.random.fold_in(jax.random.fold_in(stream_key, 6), axis_at), (shards_of,), jnp.float32, smallest / len(cuts), high / len(cuts))
        loudness = loudness * jnp.repeat(jnp.exp(heights), shape[axis_at] // shards_of).reshape((-1,) + (1,) * (len(shape) - 1 - axis_at))
    return loudness


def gaussian(key, dims, deviation, limit, shards=(), kind=jnp.bfloat16):
    loudness = block_scale(key, dims, shards, -0.22, 0.18) if shards else 1.0
    result = jax.random.normal(key, dims, jnp.float32) * deviation * loudness
    return jnp.minimum(jnp.maximum(result, -limit), limit).astype(kind)


def setup_inputs(seed: int = 0) -> dict:
    streams_of = jax.random.split(jax.random.key(seed), 7)
    return {
        "right_side": gaussian(streams_of[0], (RHS, POINTS), 1.0, 6.0, ((1, 128),), jnp.float32),
        "point_order": jax.vmap(lambda own: jax.random.permutation(own, PTS_DEV))(jax.random.split(streams_of[1], DEVICES)).reshape((DEVICES, PTS_DEV)).astype(jnp.int32),
        "noise_var": jnp.clip(jnp.exp(math.log(1.0) - 2.3025851 * jax.random.uniform(streams_of[2], (POINTS,), jnp.float32) ** block_scale(streams_of[2], (POINTS,), ((0, 128),), -0.2, 0.2)), 0.1, 1.0),
        "block_pairs": draw_block_pairs(jax.random.fold_in(streams_of[6], 71), 0),
        "pair_blocks": draw_pair_blocks(jax.random.fold_in(streams_of[6], 71), 0),
        "diag_blocks": draw_diag_blocks(jax.random.fold_in(streams_of[6], 71), 0),
    }


def apply_operator(vector, noise_var, block_pairs, pair_blocks, diag_blocks):
    rounded = lax.optimization_barrier(vector.astype(jnp.bfloat16)).astype(jnp.float32)
    by_block = rounded.reshape(RHS, BLOCKS, BLOCK)
    diag_part = jnp.einsum("bij,rbj->rbi", diag_blocks.astype(jnp.float32), by_block)
    row_ids = block_pairs[:, 0].reshape(DEVICES, PAIR_DEV)
    col_ids = block_pairs[:, 1].reshape(DEVICES, PAIR_DEV)
    kernels = pair_blocks.reshape(DEVICES, PAIR_DEV, BLOCK, BLOCK)

    def add_group(carried, group_data):
        rows_here, cols_here, kernel_here = group_data
        live_weight = (rows_here >= 0).astype(jnp.float32)[None, :, None]
        row_safe = jnp.maximum(rows_here, 0).astype(jnp.int32)
        col_safe = jnp.maximum(cols_here, 0).astype(jnp.int32)
        kernel_float = kernel_here.astype(jnp.float32)
        to_rows = jnp.einsum("pij,rpj->rpi", kernel_float, by_block[:, col_safe]) * live_weight
        to_cols = jnp.einsum("pij,rpi->rpj", kernel_float, by_block[:, row_safe]) * live_weight
        carried = carried.at[:, row_safe].add(to_rows).at[:, col_safe].add(to_cols)
        return carried, None

    start_sum = jnp.zeros((RHS, BLOCKS, BLOCK), jnp.float32)
    pair_part, unused = lax.scan(add_group, start_sum, (row_ids, col_ids, kernels))
    return (diag_part + pair_part).reshape(RHS, POINTS) + noise_var[None, :] * vector


def reference(right_side, point_order, noise_var, block_pairs, pair_blocks, diag_blocks):
    shaped = right_side.reshape(RHS, DEVICES, PTS_DEV)
    curve_rhs = jnp.take_along_axis(shaped, point_order[None, :, :], axis=2).reshape(RHS, POINTS)
    solution = jnp.zeros_like(curve_rhs)
    residual = curve_rhs
    direction = curve_rhs
    norm_now = jnp.sum(residual * residual, axis=1)
    for iteration in range(ITERS):
        image_vec = apply_operator(direction, noise_var, block_pairs, pair_blocks, diag_blocks)
        step_size = norm_now / jnp.sum(direction * image_vec, axis=1)
        solution = solution + step_size[:, None] * direction
        residual = residual - step_size[:, None] * image_vec
        if iteration + 1 < ITERS:
            norm_next = jnp.sum(residual * residual, axis=1)
            direction = residual + (norm_next / norm_now)[:, None] * direction
            norm_now = norm_next
    return solution, residual
```

```python
import functools
import math

import jax
import jax.numpy as jnp
from jax import lax
from jax.experimental import pallas as pl
from jax.experimental.pallas import tpu as pltpu
from jax.sharding import PartitionSpec as P

ITERS = 3
UNROLL = 32
PARTS = 6
F32 = jnp.float32
BF16 = jnp.bfloat16
MESH = pl.DeviceIdType.MESH


def kernel(
    cfg,
    right_hbm,
    order_hbm,
    noise_hbm,
    pairs_hbm,
    blocks_hbm,
    diag_hbm,
    sol_ref,
    res_ref,
    right,
    order,
    noise,
    pairs,
    blocks,
    diag,
    base,
    image,
    twice,
    resid,
    direct,
    image_next,
    resid_image,
    diag_part,
    field,
    products,
    partial,
    arrived,
    ahead,
    table_vec,
    table,
    sums,
    in_sem,
    blocks_sem,
    table_sem,
    field_send,
    field_recv,
    field_fwd,
    ahead_send,
    ahead_recv,
    part_send,
    part_recv,
    part_ahead_send,
    part_ahead_recv,
    sums_send,
    sums_recv,
):
    tiles, subs, side, blk_dev, block, slots, rhs = cfg
    half = blk_dev // 2
    t = lax.axis_index("tile")
    s = lax.axis_index("sub")
    core = lax.rem(t, 2)
    chip_x = lax.rem(t // 2, side)
    chip_y = t // (2 * side)
    above = lax.rem(s + 1, subs)
    below = lax.rem(s + subs - 1, subs)
    across = lax.rem(s + 2, subs)
    has_behind = t > 0
    has_ahead = t < tiles - 1

    loads = [
        pltpu.make_async_copy(right_hbm, right, in_sem.at[0]),
        pltpu.make_async_copy(order_hbm, order, in_sem.at[1]),
        pltpu.make_async_copy(pairs_hbm, pairs, in_sem.at[2]),
        pltpu.make_async_copy(noise_hbm, noise, in_sem.at[3]),
        pltpu.make_async_copy(diag_hbm, diag, in_sem.at[4]),
    ]
    step = slots // PARTS
    block_loads = [
        pltpu.make_async_copy(
            blocks_hbm.at[pl.ds(i * step, step)],
            blocks.at[pl.ds(i * step, step)],
            blocks_sem.at[i],
        )
        for i in range(PARTS)
    ]

    group1 = core * subs + s

    def partner1(index):
        return (t - core + index // subs, lax.rem(index, subs))

    def partner2(index):
        return ((chip_y * side + index) * 2 + core, s)

    def partner3(index):
        return ((index * side + chip_x) * 2 + core, s)

    stages = (
        (2 * subs, group1, partner1, 0),
        (side, chip_x, partner2, 2 * subs),
        (side, chip_y, partner3, 2 * subs + side),
    )

    barrier = pltpu.get_barrier_semaphore()
    greeted = 0
    for count, mine, partner, unused in stages:
        for j in range(1, count):
            pl.semaphore_signal(
                barrier, inc=1, device_id=partner(lax.rem(mine + j, count)), device_id_type=MESH
            )
            greeted += 1
    far_ahead = (core == 1) & has_ahead
    far_behind = (core == 0) & has_behind

    @pl.when(far_ahead)
    def _():
        pl.semaphore_signal(barrier, inc=1, device_id=(t + 1, s), device_id_type=MESH)

    @pl.when(far_behind)
    def _():
        pl.semaphore_signal(barrier, inc=1, device_id=(t - 1, s), device_id_type=MESH)

    for copy in loads:
        copy.start()
    for copy in block_loads:
        copy.start()

    loads[0].wait()
    loads[1].wait()
    lanes = 128
    chunks = right.shape[1] // lanes

    def permute(i, carry):
        at = pl.multiple_of(i * lanes, lanes)
        index = jnp.broadcast_to(order[:, pl.ds(at, lanes)], (rhs, lanes))
        low = lax.bitwise_and(index, lanes - 1)
        high = lax.shift_right_logical(index, 7)
        out = jnp.zeros((rhs, lanes), F32)
        for h in range(chunks):
            picked = jnp.take_along_axis(right[:, h * lanes : (h + 1) * lanes], low, axis=1)
            out = jnp.where(high == h, picked, out)
        base[:, pl.ds(at, lanes)] = out
        return carry

    lax.fori_loop(0, chunks, permute, 0)

    def put_field(k, values):
        for b in range(blk_dev):
            field[k, s * blk_dev + b] = values[:, b * block : (b + 1) * block].astype(BF16)

    def field_half(k, row, h):
        return field.at[k, pl.ds(row * blk_dev + h * half, half)]

    def field_copy(k, row, h, target, send):
        return pltpu.make_async_remote_copy(
            src_ref=field_half(k, row, h),
            dst_ref=field_half(k, row, h),
            send_sem=send,
            recv_sem=field_recv.at[k, row, h],
            device_id=(t, target),
            device_id_type=MESH,
        )

    def ahead_copy(k, h):
        return pltpu.make_async_remote_copy(
            src_ref=field_half(k, 0, h),
            dst_ref=field_half(k, subs, h),
            send_sem=ahead_send.at[k, h],
            recv_sem=ahead_recv.at[k, h],
            device_id=(t - 1, s),
            device_id_type=MESH,
        )

    def pass_back(k, row, h):
        @pl.when((row == 0) & has_behind)
        def _():
            ahead_copy(k, h).start()

    def start_field(k):
        for target, h, n in ((above, 0, 0), (below, 1, 1), (above, 1, 2), (below, 0, 3)):
            field_copy(k, s, h, target, field_send.at[k, n]).start()
        for h in range(2):
            pass_back(k, s, h)

    def finish_field(k):
        field_copy(k, below, 0, s, field_send.at[k, 0]).wait_recv()
        field_copy(k, below, 0, above, field_fwd.at[k, 0]).start()
        pass_back(k, below, 0)
        field_copy(k, above, 1, s, field_send.at[k, 0]).wait_recv()
        field_copy(k, above, 1, below, field_fwd.at[k, 1]).start()
        pass_back(k, above, 1)
        for row, h in ((below, 1), (above, 0), (across, 0), (across, 1)):
            field_copy(k, row, h, s, field_send.at[k, 0]).wait_recv()
            pass_back(k, row, h)

        @pl.when(has_ahead)
        def _():
            for h in range(2):
                ahead_copy(k, h).wait_recv()

    def drain_field(k):
        for target, h, n in ((above, 0, 0), (below, 1, 1), (above, 1, 2), (below, 0, 3)):
            field_copy(k, s, h, target, field_send.at[k, n]).wait_send()
        field_copy(k, below, 0, above, field_fwd.at[k, 0]).wait_send()
        field_copy(k, above, 1, below, field_fwd.at[k, 1]).wait_send()

        @pl.when(has_behind)
        def _():
            for h in range(2):
                ahead_copy(k, h).wait_send()

    def sums_copy(k, stage, j):
        count, mine, partner, offset = stages[stage]
        other = lax.rem(mine + j, count)
        return pltpu.make_async_remote_copy(
            src_ref=sums.at[k, offset + mine],
            dst_ref=sums.at[k, offset + mine],
            send_sem=sums_send.at[k, offset + j],
            recv_sem=sums_recv.at[k, offset + mine],
            device_id=partner(other),
            device_id_type=MESH,
        )

    def sums_start(k, stage, values):
        count, mine, partner, offset = stages[stage]
        sums[k, offset + mine] = values
        for j in range(1, count):
            sums_copy(k, stage, j).start()

    def sums_finish(k, stage):
        count, mine, partner, offset = stages[stage]
        for j in range(1, count):
            other = lax.rem(mine + j, count)
            pltpu.make_async_remote_copy(
                src_ref=sums.at[k, offset + other],
                dst_ref=sums.at[k, offset + other],
                send_sem=sums_send.at[k, offset + j],
                recv_sem=sums_recv.at[k, offset + other],
                device_id=partner(other),
                device_id_type=MESH,
            ).wait_recv()
        total = sums[k, offset]
        for j in range(1, count):
            total = total + sums[k, offset + j]
        return total

    def sums_drain(k):
        for stage in range(3):
            for j in range(1, stages[stage][0]):
                sums_copy(k, stage, j).wait_send()

    def fold(values):
        parts = [values[:, i * lanes : (i + 1) * lanes] for i in range(chunks)]
        while len(parts) > 1:
            parts = [a + b for a, b in zip(parts[::2], parts[1::2])]
        return parts[0]

    def pack(*values):
        folded = [fold(v) for v in values]
        while len(folded) < 3:
            folded.append(jnp.zeros_like(folded[0]))
        return jnp.stack(folded)

    def scalar(total, n):
        return jnp.sum(total[n], axis=1, keepdims=True)

    first = t * (subs * blk_dev)

    def row_of(p):
        return jnp.maximum(pairs[0, p] - first, 0)

    def col_of(p):
        return jnp.maximum(pairs[1, p] - first, 0)

    def build_table():
        shape = (8, lanes)
        ids = lax.broadcasted_iota(jnp.int32, shape, 0) * lanes + lax.broadcasted_iota(
            jnp.int32, shape, 1
        )

        def add_slot(i, found):
            for u in range(8):
                p = i * 8 + u
                row = pairs[0, p]
                col = pairs[1, p]
                apart = col - row
                kind = jnp.where(apart == 1, 0, apart - (blk_dev - 2))
                live = row >= 0
                key_col = jnp.where(live, (col - first) * 8 + kind, -1)
                key_row = jnp.where(live, (row - first) * 8 + 4 + kind, -1)
                found = jnp.where(ids == key_col, p + 1, found)
                found = jnp.where(ids == key_row, p + 1 + slots, found)
            return found

        table_vec[...] = lax.fori_loop(0, slots // 8, add_slot, jnp.zeros(shape, jnp.int32))
        move = pltpu.make_async_copy(table_vec, table, table_sem)
        move.start()
        move.wait()
        products[0] = jnp.zeros((rhs, block), F32)

    def diag_products(k):
        def body(i, carry):
            for u in range(4):
                b = i * 4 + u
                at = pl.multiple_of(b * block, block)
                diag_part[:, pl.ds(at, block)] = jnp.dot(
                    field[k, s * blk_dev + b], diag[b], preferred_element_type=F32
                )
            return carry

        lax.fori_loop(0, blk_dev // 4, body, 0)

    def pair_products(k, low, high):
        def body(i, carry):
            for u in range(UNROLL):
                p = i * UNROLL + u
                kernel_block = blocks[p]
                products[1 + p] = lax.dot_general(
                    field[k, row_of(p)],
                    kernel_block,
                    (((1,), (0,)), ((), ())),
                    preferred_element_type=F32,
                )
                products[1 + slots + p] = lax.dot_general(
                    field[k, col_of(p)],
                    kernel_block,
                    (((1,), (1,)), ((), ())),
                    preferred_element_type=F32,
                )
            return carry

        lax.fori_loop(low, high, body, 0)

    def gathered_sum(row, b):
        at = (row * blk_dev + b) * 8
        total = products[table[at // lanes, lax.rem(at, lanes)]]
        for n in range(1, 8):
            total = total + products[table[at // lanes, lax.rem(at, lanes) + n]]
        return total

    def fill_partial(k, row, n, with_ahead):
        def body(i, carry):
            for u in range(4):
                b = i * 4 + u
                total = gathered_sum(row, b)
                if with_ahead:
                    total = total + jnp.where(row == 0, ahead[k, b].astype(F32), 0.0)
                partial[k, n, b] = total.astype(BF16)
            return carry

        lax.fori_loop(0, blk_dev // 4, body, 0)

    def part_copy(k, n, row):
        return pltpu.make_async_remote_copy(
            src_ref=partial.at[k, n],
            dst_ref=arrived.at[k, s],
            send_sem=part_send.at[k, n],
            recv_sem=part_recv.at[k, s],
            device_id=(t, row),
            device_id_type=MESH,
        )

    def part_ahead_copy(k):
        return pltpu.make_async_remote_copy(
            src_ref=partial.at[k, 3],
            dst_ref=ahead.at[k],
            send_sem=part_ahead_send.at[k],
            recv_sem=part_ahead_recv.at[k],
            device_id=(t + 1, s),
            device_id_type=MESH,
        )

    rows = (
        jnp.where(s == 1, 2, 1),
        jnp.where((s == 0) | (s == 3), 2, 3),
        jnp.where(s == 0, 3, 0),
    )

    def send_products(k):
        @pl.when(has_ahead)
        def _():
            fill_partial(k, subs, 3, False)
            part_ahead_copy(k).start()

        for n in range(2):
            fill_partial(k, rows[n], n, False)
            part_copy(k, n, rows[n]).start()

        @pl.when(has_behind)
        def _():
            part_ahead_copy(k).wait_recv()

        fill_partial(k, rows[2], 2, True)
        part_copy(k, 2, rows[2]).start()

    def take_products(k, vector, out):
        own = jnp.where(s == 0, 1.0, 0.0).astype(F32)

        def body(i, carry):
            for u in range(4):
                b = i * 4 + u
                at = pl.ds(pl.multiple_of(b * block, block), block)
                total = gathered_sum(s, b) + diag_part[:, at]
                diag_part[:, at] = total + jnp.where(s == 0, ahead[k, b].astype(F32), 0.0)
            return carry

        lax.fori_loop(0, blk_dev // 4, body, 0)
        for j in range(1, subs):
            other = lax.rem(s + j, subs)
            pltpu.make_async_remote_copy(
                src_ref=partial.at[k, 0],
                dst_ref=arrived.at[k, other],
                send_sem=part_send.at[k, 0],
                recv_sem=part_recv.at[k, other],
                device_id=(t, other),
                device_id_type=MESH,
            ).wait_recv()
        others = [lax.rem(s + j, subs) for j in range(1, subs)]

        def combine(i, carry):
            for u in range(4):
                b = i * 4 + u
                at = pl.ds(pl.multiple_of(b * block, block), block)
                total = arrived[k, others[0], b].astype(F32)
                for other in others[1:]:
                    total = total + arrived[k, other, b].astype(F32)
                out[:, at] = total + (diag_part[:, at] + noise[:, at] * vector[:, at])
            return carry

        lax.fori_loop(0, blk_dev // 4, combine, 0)

    def drain_products(k):
        for n in range(3):
            part_copy(k, n, rows[n]).wait_send()

        @pl.when(has_ahead)
        def _():
            part_ahead_copy(k).wait_send()

    trips = slots // UNROLL

    put_field(0, base[...])

    @pl.when(jnp.logical_not(has_ahead))
    def _():
        for k in range(ITERS):
            for b in range(blk_dev):
                field[k, subs * blk_dev + b] = jnp.zeros((rhs, block), BF16)

    @pl.when(jnp.logical_not(has_behind))
    def _():
        for k in range(ITERS):
            ahead[k] = jnp.zeros((blk_dev, rhs, block), BF16)

    pl.semaphore_wait(barrier, greeted + jnp.where(far_ahead | far_behind, 1, 0))
    start_field(0)
    loads[2].wait()
    build_table()
    loads[4].wait()
    diag_products(0)
    finish_field(0)
    for copy in block_loads:
        copy.wait()
    pair_products(0, 0, trips)
    send_products(0)
    loads[3].wait()
    take_products(0, base, image)

    b_now = base[...]
    q_now = image[...]
    put_field(1, q_now)
    start_field(1)
    sums_start(0, 0, pack(b_now * b_now, b_now * q_now, q_now * q_now))
    diag_products(1)
    finish_field(1)
    sums_start(0, 1, sums_finish(0, 0))
    pair_products(1, 0, 1)
    sums_start(0, 2, sums_finish(0, 1))
    pair_products(1, 1, trips)
    send_products(1)
    total = sums_finish(0, 2)
    norm0 = scalar(total, 0)
    curve0 = scalar(total, 1)
    square0 = scalar(total, 2)
    step0 = norm0 / curve0
    norm1 = norm0 - 2.0 * step0 * curve0 + step0 * step0 * square0
    mix0 = norm1 / norm0
    resid[...] = base[...] - step0 * image[...]
    direct[...] = resid[...] + mix0 * base[...]
    take_products(1, image, twice)
    resid_image[...] = image[...] - step0 * twice[...]
    image_next[...] = resid_image[...] + mix0 * image[...]

    put_field(2, image_next[...])
    start_field(2)
    q_now = image_next[...]
    sums_start(1, 0, pack(direct[...] * q_now, resid[...] * q_now, q_now * q_now))
    diag_products(2)
    finish_field(2)
    sums_start(1, 1, sums_finish(1, 0))
    pair_products(2, 0, 1)
    sums_start(1, 2, sums_finish(1, 1))
    pair_products(2, 1, trips)
    send_products(2)
    total = sums_finish(1, 2)
    curve1 = scalar(total, 0)
    cross1 = scalar(total, 1)
    square1 = scalar(total, 2)
    step1 = norm1 / curve1
    norm2 = norm1 - 2.0 * step1 * cross1 + step1 * step1 * square1
    mix1 = norm2 / norm1
    sol_ref[...] = step0 * base[...] + step1 * direct[...]
    resid[...] = resid[...] - step1 * image_next[...]
    direct[...] = resid[...] + mix1 * direct[...]
    take_products(2, image_next, twice)
    image[...] = (resid_image[...] - step1 * twice[...]) + mix1 * image_next[...]
    sums_start(2, 0, pack(direct[...] * image[...]))
    sums_start(2, 1, sums_finish(2, 0))
    sums_start(2, 2, sums_finish(2, 1))
    total = sums_finish(2, 2)
    step2 = norm2 / scalar(total, 0)
    sol_ref[...] = sol_ref[...] + step2 * direct[...]
    res_ref[...] = resid[...] - step2 * image[...]

    for k in range(ITERS):
        drain_field(k)
        drain_products(k)
        sums_drain(k)


def solution(mesh):
    tiles, subs = mesh.shape["tile"], mesh.shape["sub"]
    side = math.isqrt(tiles // 2)

    def on_device(right_side, point_order, noise_var, block_pairs, pair_blocks, diag_blocks):
        rhs, points = right_side.shape
        slots, block = pair_blocks.shape[:2]
        blk_dev = diag_blocks.shape[0]
        cfg = (tiles, subs, side, blk_dev, block, slots, rhs)
        slots_all = 2 * subs + 2 * side
        vec = pltpu.VMEM((rhs, points), F32)
        dma = pltpu.SemaphoreType.DMA
        return pl.pallas_call(
            functools.partial(kernel, cfg),
            out_shape=(jax.ShapeDtypeStruct((rhs, points), F32),) * 2,
            in_specs=[pl.BlockSpec(memory_space=pl.ANY)] * 6,
            out_specs=(pl.BlockSpec(memory_space=pltpu.VMEM),) * 2,
            scratch_shapes=[
                vec,
                pltpu.VMEM((1, points), jnp.int32),
                pltpu.VMEM((1, points), F32),
                pltpu.SMEM((2, slots), jnp.int32),
                pltpu.VMEM((slots, block, block), BF16),
                pltpu.VMEM((blk_dev, block, block), BF16),
                vec,
                vec,
                vec,
                vec,
                vec,
                vec,
                vec,
                vec,
                pltpu.VMEM((ITERS, (subs + 1) * blk_dev, rhs, block), BF16),
                pltpu.VMEM((1 + 2 * slots, rhs, block), F32),
                pltpu.VMEM((ITERS, 4, blk_dev, rhs, block), BF16),
                pltpu.VMEM((ITERS, subs, blk_dev, rhs, block), BF16),
                pltpu.VMEM((ITERS, blk_dev, rhs, block), BF16),
                pltpu.VMEM((8, 128), jnp.int32),
                pltpu.SMEM((8, 128), jnp.int32),
                pltpu.VMEM((ITERS, slots_all, 3, rhs, 128), F32),
                dma((5,)),
                dma((PARTS,)),
                dma,
                dma((ITERS, 4)),
                dma((ITERS, subs, 2)),
                dma((ITERS, 2)),
                dma((ITERS, 2)),
                dma((ITERS, 2)),
                dma((ITERS, 3)),
                dma((ITERS, subs)),
                dma((ITERS,)),
                dma((ITERS,)),
                dma((ITERS, slots_all)),
                dma((ITERS, slots_all)),
            ],
            compiler_params=pltpu.CompilerParams(
                collective_id=0, has_side_effects=True, vmem_limit_bytes=40 << 20
            ),
            name="block_pair_solve",
        )(
            right_side,
            point_order,
            noise_var.reshape(1, -1),
            block_pairs.T,
            pair_blocks,
            diag_blocks,
        )

    both = ("tile", "sub")
    return jax.shard_map(
        on_device,
        mesh=mesh,
        in_specs=(
            P(None, both),
            P(both, None),
            P(both),
            P(both, None),
            P(both, None, None),
            P(both, None, None),
        ),
        out_specs=(P(None, both), P(None, both)),
        check_vma=False,
    )
```

```python
import functools
import math

import jax
import jax.numpy as jnp
from jax import lax
from jax.experimental import pallas as pl
from jax.experimental.pallas import tpu as pltpu
from jax.sharding import PartitionSpec as P

ITERS = 3
UNROLL = 24
PARTS = 6
LANES = 128
F32 = jnp.float32
BF16 = jnp.bfloat16
MESH = pl.DeviceIdType.MESH


def scope(name):
    return jax.named_scope(name)


def kernel(
    cfg,
    right_hbm,
    order_hbm,
    noise_hbm,
    pairs_hbm,
    blocks_hbm,
    diag_hbm,
    sol_ref,
    res_ref,
    right,
    order,
    noise,
    pairs,
    blocks,
    diag,
    base,
    image,
    twice,
    resid,
    direct,
    image_next,
    resid_image,
    own_part,
    field,
    field_ahead,
    products,
    parts_out,
    parts_in,
    to_ahead,
    from_behind,
    table_vec,
    table,
    sums,
    in_sem,
    blocks_sem,
    table_sem,
    field_send,
    field_recv,
    ahead_send,
    ahead_recv,
    part_send,
    part_recv,
    behind_send,
    behind_recv,
    sums_send,
    sums_recv,
):
    tiles, subs, side, blk_dev, block, slots, rhs = cfg
    half = blk_dev // 2
    t = lax.axis_index("tile")
    s = lax.axis_index("sub")
    core = lax.rem(t, 2)
    above = lax.rem(s + 1, subs)
    below = lax.rem(s + subs - 1, subs)
    across = lax.rem(s + 2, subs)
    has_behind = t > 0
    has_ahead = t < tiles - 1

    loads = [
        pltpu.make_async_copy(right_hbm, right, in_sem.at[0]),
        pltpu.make_async_copy(order_hbm, order, in_sem.at[1]),
        pltpu.make_async_copy(pairs_hbm, pairs, in_sem.at[2]),
        pltpu.make_async_copy(noise_hbm, noise, in_sem.at[3]),
        pltpu.make_async_copy(diag_hbm, diag, in_sem.at[4]),
    ]
    step = slots // PARTS
    block_loads = [
        pltpu.make_async_copy(
            blocks_hbm.at[pl.ds(i * step, step)],
            blocks.at[pl.ds(i * step, step)],
            blocks_sem.at[i],
        )
        for i in range(PARTS)
    ]
    group = core * subs + s
    chip_x = lax.rem(t // 2, side)
    chip_y = t // (2 * side)

    def column_partner(index):
        return (t - core + index // subs, lax.rem(index, subs))

    def x_partner(index):
        return ((chip_y * side + index) * 2 + core, s)

    def y_partner(index):
        return ((index * side + chip_x) * 2 + core, s)

    stages = (
        (2 * subs, group, column_partner, 0),
        (side, chip_x, x_partner, 2 * subs),
        (side, chip_y, y_partner, 2 * subs + side),
    )

    barrier = pltpu.get_barrier_semaphore()
    greeted = 0
    for count, mine, partner, unused in stages:
        for j in range(1, count):
            pl.semaphore_signal(
                barrier, inc=1, device_id=partner(lax.rem(mine + j, count)), device_id_type=MESH
            )
            greeted += 1
    far_ahead = (core == 1) & has_ahead
    far_behind = (core == 0) & has_behind

    @pl.when(far_ahead)
    def _():
        pl.semaphore_signal(barrier, inc=1, device_id=(t + 1, s), device_id_type=MESH)

    @pl.when(far_behind)
    def _():
        pl.semaphore_signal(barrier, inc=1, device_id=(t - 1, s), device_id_type=MESH)

    for copy in loads[:2]:
        copy.start()
    for copy in block_loads[:1]:
        copy.start()
    for copy in loads[2:]:
        copy.start()
    for copy in block_loads[1:]:
        copy.start()

    chunks = right.shape[1] // LANES

    def permute(i, carry):
        at = pl.multiple_of(i * LANES, LANES)
        index = jnp.broadcast_to(order[:, pl.ds(at, LANES)], (rhs, LANES))
        low = lax.bitwise_and(index, LANES - 1)
        high = lax.shift_right_logical(index, 7)
        out = jnp.zeros((rhs, LANES), F32)
        for h in range(chunks):
            picked = jnp.take_along_axis(right[:, h * LANES : (h + 1) * LANES], low, axis=1)
            out = jnp.where(high == h, picked, out)
        base[:, pl.ds(at, LANES)] = out
        return carry

    def put_field(k, values, h):
        for b in range(h * half, (h + 1) * half):
            at = (b - h * half) * block
            field[k, s * blk_dev + b] = values[:, at : at + block].astype(BF16)

    def pieces(k):
        return 2 if k == 0 else 1

    def field_piece(k, row, h):
        length = blk_dev // pieces(k)
        return field.at[k, pl.ds(row * blk_dev + h * length, length)]

    targets = (across, above, below)
    sources = (across, below, above)

    def field_copy(k, row, h, n):
        return pltpu.make_async_remote_copy(
            src_ref=field_piece(k, row, h),
            dst_ref=field_piece(k, row, h),
            send_sem=field_send.at[k, n, h],
            recv_sem=field_recv.at[k, row, h],
            device_id=(t, targets[n]),
            device_id_type=MESH,
        )

    def ahead_copy(k, h):
        length = blk_dev // pieces(k)
        return pltpu.make_async_remote_copy(
            src_ref=field_piece(k, 0, h),
            dst_ref=field_ahead.at[k, pl.ds(h * length, length)],
            send_sem=ahead_send.at[k, h],
            recv_sem=ahead_recv.at[k, h],
            device_id=(t - 1, s),
            device_id_type=MESH,
        )

    def pass_back(k, row, h):
        @pl.when((row == 0) & has_behind)
        def _():
            ahead_copy(k, h).start()

    def start_field(k, h):
        for n in range(3):
            field_copy(k, s, h, n).start()
        pass_back(k, s, h)

    def finish_field(k):
        for h in range(pieces(k)):
            for n in (1, 2, 0):
                field_copy(k, sources[n], h, n).wait_recv()
                pass_back(k, sources[n], h)

    def finish_ahead(k):
        @pl.when(has_ahead)
        def _():
            for h in range(pieces(k)):
                ahead_copy(k, h).wait_recv()

        for b in range(blk_dev):
            field[k, subs * blk_dev + b] = field_ahead[k, b]

    def drain_field(k):
        for h in range(pieces(k)):
            for n in range(3):
                field_copy(k, s, h, n).wait_send()

        @pl.when(has_behind)
        def _():
            for h in range(pieces(k)):
                ahead_copy(k, h).wait_send()

    def sums_copy(k, stage, j, incoming):
        count, mine, partner, offset = stages[stage]
        other = lax.rem(mine + j, count)
        at = offset + (other if incoming else mine)
        return pltpu.make_async_remote_copy(
            src_ref=sums.at[k, at],
            dst_ref=sums.at[k, at],
            send_sem=sums_send.at[k, offset + j],
            recv_sem=sums_recv.at[k, at],
            device_id=partner(other),
            device_id_type=MESH,
        )

    def sums_start(k, stage, values):
        count, mine, partner, offset = stages[stage]
        sums[k, offset + mine] = values
        for j in range(1, count):
            sums_copy(k, stage, j, False).start()

    def sums_finish(k, stage):
        count, mine, partner, offset = stages[stage]
        for j in range(1, count):
            sums_copy(k, stage, j, True).wait_recv()
        total = sums[k, offset]
        for j in range(1, count):
            total = total + sums[k, offset + j]
        return total

    def sums_drain(k):
        for stage in range(3):
            for j in range(1, stages[stage][0]):
                sums_copy(k, stage, j, False).wait_send()

    def fold(values):
        parts = [values[:, i : i + LANES] for i in range(0, values.shape[1], LANES)]
        while len(parts) > 1:
            parts = [a + b for a, b in zip(parts[::2], parts[1::2])]
        return parts[0]

    spot = lax.broadcasted_iota(jnp.int32, (rhs, LANES), 1) - lax.broadcasted_iota(
        jnp.int32, (rhs, LANES), 0
    )

    def pack(*folded):
        out = jnp.zeros((rhs, LANES), F32)
        for n, values in enumerate(folded):
            column = jnp.sum(values, axis=1, keepdims=True)
            out = jnp.where(spot == n * rhs, column, out)
        return jnp.sum(out, axis=0, keepdims=True)

    def unpack(total, n):
        wide = jnp.broadcast_to(total, (rhs, LANES))
        return jnp.sum(jnp.where(spot == n * rhs, wide, 0.0), axis=1, keepdims=True)

    first = t * (subs * blk_dev)
    tile_blocks = subs * blk_dev

    def build_table():
        shape = (8, LANES)
        sub_id = lax.broadcasted_iota(jnp.int32, shape, 0)
        lane_id = lax.broadcasted_iota(jnp.int32, shape, 1)
        ids = sub_id * LANES + lane_id

        def add_slot(i, carry):
            found, listed, low, high = carry
            for u in range(8):
                p = i * 8 + u
                row = pairs[0, p]
                col = pairs[1, p]
                live = row >= 0
                reach = jnp.where(col - first >= tile_blocks, 1, 0)
                place = jnp.where(reach == 1, low, high)
                low = low + reach
                high = high - (1 - reach)
                apart = col - row
                kind = jnp.where(apart == 1, 0, apart - (blk_dev - 2))
                key_col = jnp.where(live, (col - first) * 8 + kind, -1)
                key_row = jnp.where(live, (row - first) * 8 + 4 + kind, -1)
                found = jnp.where(ids == key_col, place + 1, found)
                found = jnp.where(ids == key_row, place + 1 + slots, found)
                entry = jnp.where(
                    sub_id == 0,
                    p,
                    jnp.where(
                        sub_id == 1, jnp.maximum(row - first, 0), jnp.maximum(col - first, 0)
                    ),
                )
                listed = jnp.where(lane_id == place, entry, listed)
            return found, listed, low, high

        zeros = jnp.zeros(shape, jnp.int32)
        found, listed, unused_low, unused_high = lax.fori_loop(
            0, slots // 8, add_slot, (zeros, zeros, jnp.int32(0), jnp.int32(slots - 1))
        )
        table_vec[0:8] = found
        table_vec[8:16] = listed
        move = pltpu.make_async_copy(table_vec, table, table_sem)
        move.start()
        move.wait()
        products[0] = jnp.zeros((rhs, block), F32)

    def diag_products(k):
        def body(i, carry):
            for u in range(8):
                b = i * 8 + u
                at = pl.multiple_of(b * block, block)
                own_part[:, pl.ds(at, block)] = jnp.dot(
                    field[k, s * blk_dev + b], diag[b], preferred_element_type=F32
                )
            return carry

        lax.fori_loop(0, blk_dev // 8, body, 0)

    def col_products(k, low, high):
        def body(i, carry):
            for u in range(UNROLL):
                p = i * UNROLL + u
                products[1 + p] = lax.dot_general(
                    field[k, table[9, p]],
                    blocks[table[8, p]],
                    (((1,), (0,)), ((), ())),
                    preferred_element_type=F32,
                )
            return carry

        lax.fori_loop(low // UNROLL, high // UNROLL, body, 0)

    def row_products(k, low, high):
        def body(i, carry):
            for u in range(UNROLL):
                p = i * UNROLL + u
                products[1 + slots + p] = lax.dot_general(
                    field[k, table[10, p]],
                    blocks[table[8, p]],
                    (((1,), (1,)), ((), ())),
                    preferred_element_type=F32,
                )
            return carry

        lax.fori_loop(low // UNROLL, high // UNROLL, body, 0)

    def quadratic(k):
        def body(i, total):
            for u in range(8):
                p = i * 8 + u
                total = total + products[1 + p] * field[k, table[10, p]].astype(F32)
            return total

        return fold(lax.fori_loop(0, slots // 8, body, jnp.zeros((rhs, block), F32)))

    def gathered_sum(row, b, kinds):
        at = (row * blk_dev + b) * 8
        line = at // LANES
        lane = lax.rem(at, LANES)
        parts = [products[table[line, lane + n]] for n in kinds]
        while len(parts) > 1:
            pairs_of = [x + y for x, y in zip(parts[::2], parts[1::2])]
            parts = pairs_of + parts[len(pairs_of) * 2 :]
        return parts[0]

    def partial_sum(k, row, b):
        behind = jnp.where(row == 0, from_behind[k, b].astype(F32), 0.0)
        return gathered_sum(row, b, range(8)) + behind

    def remote(src, dst, send, recv, target):
        return pltpu.make_async_remote_copy(
            src_ref=src,
            dst_ref=dst,
            send_sem=send,
            recv_sem=recv,
            device_id=target,
            device_id_type=MESH,
        )

    def part_copy(k, n):
        return remote(
            parts_out.at[k, n], parts_in.at[k, n], part_send.at[k, n], part_recv.at[k, n], (t, targets[n])
        )

    def behind_copy(k):
        return remote(
            to_ahead.at[k],
            from_behind.at[k],
            behind_send.at[k],
            behind_recv.at[k],
            (t + 1, s),
        )

    def send_ahead(k):
        @pl.when(has_ahead)
        def _():
            def body(i, carry):
                for u in range(8):
                    b = i * 8 + u
                    to_ahead[k, b] = gathered_sum(subs, b, (1, 2, 3)).astype(BF16)
                return carry

            lax.fori_loop(0, blk_dev // 8, body, 0)
            behind_copy(k).start()

    def send_products(k):
        @pl.when(has_behind)
        def _():
            behind_copy(k).wait_recv()

        for n in range(3):

            def body(i, carry):
                for u in range(8):
                    b = i * 8 + u
                    parts_out[k, n, b] = partial_sum(k, targets[n], b).astype(BF16)
                return carry

            lax.fori_loop(0, blk_dev // 8, body, 0)
            part_copy(k, n).start()

    def own_products(k):
        def body(i, carry):
            for u in range(4):
                b = i * 4 + u
                at = pl.ds(pl.multiple_of(b * block, block), block)
                own_part[:, at] = own_part[:, at] + partial_sum(k, s, b)
            return carry

        lax.fori_loop(0, blk_dev // 4, body, 0)

    def take_products(k, vector, out):
        for n in (1, 2, 0):
            part_copy(k, n).wait_recv()
        for b in range(blk_dev):
            at = slice(b * block, (b + 1) * block)
            total = parts_in[k, 0, b].astype(F32) + parts_in[k, 1, b].astype(F32)
            total = total + parts_in[k, 2, b].astype(F32)
            out[:, at] = total + (own_part[:, at] + noise[:, at] * vector[:, at])

    def drain_products(k):
        for n in range(3):
            part_copy(k, n).wait_send()

        @pl.when(has_ahead)
        def _():
            behind_copy(k).wait_send()

    middle = slots // 2

    loads[0].wait()
    loads[1].wait()
    with scope("permute0"):
        lax.fori_loop(0, chunks // 2, permute, 0)
        put_field(0, base[:, 0 : half * block], 0)
    with scope("barrier"):
        pl.semaphore_wait(barrier, greeted + jnp.where(far_ahead | far_behind, 1, 0))
    start_field(0, 0)
    with scope("permute1"):
        lax.fori_loop(chunks // 2, chunks, permute, 0)
        put_field(0, base[:, half * block :], 1)
    start_field(0, 1)

    @pl.when(jnp.logical_not(has_ahead))
    def _():
        for k in range(ITERS):
            field_ahead[k] = jnp.zeros((blk_dev, rhs, block), BF16)

    @pl.when(jnp.logical_not(has_behind))
    def _():
        for k in range(ITERS):
            from_behind[k] = jnp.zeros((blk_dev, rhs, block), BF16)

    loads[2].wait()
    with scope("table"):
        build_table()
    loads[4].wait()
    with scope("diag0"):
        diag_products(0)
    with scope("finish0"):
        finish_field(0)
    for copy in block_loads:
        copy.wait()
    with scope("cols0"):
        col_products(0, 0, middle)
        send_ahead(0)
        col_products(0, middle, slots)
    with scope("rows0"):
        row_products(0, middle, slots)
        finish_ahead(0)
        row_products(0, 0, middle)
    with scope("send0"):
        send_products(0)
    with scope("own0"):
        own_products(0)
    loads[3].wait()
    with scope("take0"):
        take_products(0, base, image)

    with scope("start1"):
        put_field(1, image[:, 0 : half * block], 0)
        put_field(1, image[:, half * block :], 1)
        start_field(1, 0)
    with scope("sums0"):
        b_now = base[...]
        q_now = image[...]
        sums_start(0, 0, pack(fold(b_now * b_now), fold(b_now * q_now), fold(q_now * q_now)))
    with scope("diag1"):
        diag_products(1)
    with scope("finish1"):
        finish_field(1)
    with scope("sums0b"):
        sums_start(0, 1, sums_finish(0, 0))
    with scope("cols1"):
        col_products(1, 0, middle)
        send_ahead(1)
        col_products(1, middle, slots)
    with scope("sums0c"):
        sums_start(0, 2, sums_finish(0, 1))
    with scope("rows1"):
        row_products(1, middle, slots)
        finish_ahead(1)
        row_products(1, 0, middle)
    with scope("send1"):
        send_products(1)
    with scope("own1"):
        own_products(1)
    with scope("sums0d"):
        total = sums_finish(0, 2)
        norm0 = unpack(total, 0)
        curve0 = unpack(total, 1)
        square0 = unpack(total, 2)
        step0 = norm0 / curve0
        rate0 = curve0 / norm0
        norm1 = norm0 - 2.0 * step0 * curve0 + step0 * step0 * square0
        mix0 = norm1 / norm0
        resid[...] = base[...] - step0 * image[...]
        direct[...] = resid[...] + mix0 * base[...]
    with scope("take1"):
        take_products(1, image, twice)

    with scope("start2"):
        resid_image[...] = image[...] - step0 * twice[...]
        image_next[...] = resid_image[...] + mix0 * image[...]
        image[...] = image_next[...] - rate0 * resid[...]
        put_field(2, image[:, 0 : half * block], 0)
        put_field(2, image[:, half * block :], 1)
        start_field(2, 0)
    with scope("sums1"):
        q_now = image_next[...]
        sums_start(
            1,
            0,
            pack(
                fold(direct[...] * q_now),
                fold(resid[...] * q_now),
                fold(q_now * q_now),
                fold(resid[...] * resid_image[...]),
                fold(q_now * resid_image[...]),
            ),
        )
    with scope("diag2"):
        diag_products(2)
        w_now = image[...]
        local = fold(w_now * (own_part[...] + noise[...] * w_now))
    with scope("finish2"):
        finish_field(2)
    with scope("sums1b"):
        sums_start(1, 1, sums_finish(1, 0))
    with scope("cols2"):
        col_products(2, 0, middle)
        send_ahead(2)
        col_products(2, middle, slots)
        finish_ahead(2)
    with scope("sums2"):
        sums_start(2, 0, pack(local + 2.0 * quadratic(2)))
        sums_start(1, 2, sums_finish(1, 1))
    with scope("rows2"):
        row_products(2, 0, slots)
    with scope("sums2b"):
        sums_start(2, 1, sums_finish(2, 0))
    with scope("send2"):
        send_products(2)
    with scope("own2"):
        own_products(2)
    with scope("sums2c"):
        sums_start(2, 2, sums_finish(2, 1))
    with scope("sums2d"):
        total = sums_finish(1, 2)
        curve1 = unpack(total, 0)
        cross1 = unpack(total, 1)
        square1 = unpack(total, 2)
        inner_rr = unpack(total, 3)
        inner_qr = unpack(total, 4)
        step1 = norm1 / curve1
        norm2 = norm1 - 2.0 * step1 * cross1 + step1 * step1 * square1
        mix1 = norm2 / norm1
        keep = 1.0 - step1 * rate0
        inner_ww = unpack(sums_finish(2, 2), 0)
        inner_wr = inner_qr - rate0 * inner_rr
        inner_wq = square1 - rate0 * cross1
        curve2 = (
            step1 * step1 * inner_ww
            + keep * keep * inner_rr
            + mix1 * mix1 * curve1
            - 2.0 * keep * step1 * inner_wr
            + 2.0 * keep * mix1 * cross1
            - 2.0 * step1 * mix1 * inner_wq
        )
        step2 = norm2 / curve2
        r_now = resid[...] - step1 * image_next[...]
        d_now = r_now + mix1 * direct[...]
        sol_ref[...] = step0 * base[...] + step1 * direct[...] + step2 * d_now
        resid[...] = r_now - step2 * (keep * resid_image[...] + mix1 * image_next[...])
    with scope("take2"):
        take_products(2, image, twice)
        res_ref[...] = resid[...] + (step2 * step1) * twice[...]

    with scope("drain"):
        for k in range(ITERS):
            drain_field(k)
            drain_products(k)
            sums_drain(k)


def solution(mesh):
    tiles, subs = mesh.shape["tile"], mesh.shape["sub"]
    side = math.isqrt(tiles // 2)

    def on_device(right_side, point_order, noise_var, block_pairs, pair_blocks, diag_blocks):
        rhs, points = right_side.shape
        slots, block = pair_blocks.shape[:2]
        blk_dev = diag_blocks.shape[0]
        cfg = (tiles, subs, side, blk_dev, block, slots, rhs)
        members = 2 * subs + 2 * side
        vec = pltpu.VMEM((rhs, points), F32)
        row = pltpu.VMEM((ITERS, blk_dev, rhs, block), BF16)
        dma = pltpu.SemaphoreType.DMA
        return pl.pallas_call(
            functools.partial(kernel, cfg),
            out_shape=(jax.ShapeDtypeStruct((rhs, points), F32),) * 2,
            in_specs=[pl.BlockSpec(memory_space=pltpu.MemorySpace.HBM)] * 6,
            out_specs=(pl.BlockSpec(memory_space=pltpu.VMEM),) * 2,
            scratch_shapes=[
                vec,
                pltpu.VMEM((1, points), jnp.int32),
                pltpu.VMEM((1, points), F32),
                pltpu.SMEM((2, slots), jnp.int32),
                pltpu.VMEM((slots, block, block), BF16),
                pltpu.VMEM((blk_dev, block, block), BF16),
                vec,
                vec,
                vec,
                vec,
                vec,
                vec,
                vec,
                vec,
                pltpu.VMEM((ITERS, (subs + 1) * blk_dev, rhs, block), BF16),
                row,
                pltpu.VMEM((1 + 2 * slots, rhs, block), F32),
                pltpu.VMEM((ITERS, 3, blk_dev, rhs, block), BF16),
                pltpu.VMEM((ITERS, 3, blk_dev, rhs, block), BF16),
                row,
                row,
                pltpu.VMEM((16, LANES), jnp.int32),
                pltpu.SMEM((16, LANES), jnp.int32),
                pltpu.VMEM((ITERS, members, 1, LANES), F32),
                dma((5,)),
                dma((PARTS,)),
                dma,
                dma((ITERS, 3, 2)),
                dma((ITERS, subs, 2)),
                dma((ITERS, 2)),
                dma((ITERS, 2)),
                dma((ITERS, 3)),
                dma((ITERS, 3)),
                dma((ITERS,)),
                dma((ITERS,)),
                dma((ITERS, members)),
                dma((ITERS, members)),
            ],
            compiler_params=pltpu.CompilerParams(
                collective_id=0, has_side_effects=True, vmem_limit_bytes=67043328
            ),
            name="block_pair_solve",
        )(
            right_side,
            point_order,
            noise_var.reshape(1, -1),
            block_pairs.T,
            pair_blocks,
            diag_blocks,
        )

    both = ("tile", "sub")
    return jax.shard_map(
        on_device,
        mesh=mesh,
        in_specs=(
            P(None, both),
            P(both, None),
            P(both),
            P(both, None),
            P(both, None, None),
            P(both, None, None),
        ),
        out_specs=(P(None, both), P(None, both)),
        check_vma=False,
    )
```

```python
import functools
import math

import jax
import jax.numpy as jnp
from jax import lax
from jax.experimental import pallas as pl
from jax.experimental.pallas import tpu as pltpu
from jax.sharding import PartitionSpec as P

ITERS = 3
PARTS = 6
LANES = 128
F32 = jnp.float32
BF16 = jnp.bfloat16
MESH = pl.DeviceIdType.MESH


def scope(name):
    return jax.named_scope(name)


def kernel(
    cfg,
    right_hbm,
    order_hbm,
    noise_hbm,
    pairs_hbm,
    blocks_hbm,
    diag_hbm,
    sol_ref,
    res_ref,
    right,
    order,
    noise,
    pairs,
    blocks,
    diag,
    base,
    image,
    twice,
    resid,
    direct,
    image_next,
    resid_image,
    own_part,
    field,
    field_ahead,
    col_out,
    row_out,
    half_sums,
    turned,
    parts_out,
    parts_in,
    to_ahead,
    from_behind,
    table_vec,
    table,
    sums,
    in_sem,
    blocks_sem,
    table_sem,
    field_send,
    field_recv,
    ahead_send,
    ahead_recv,
    part_send,
    part_recv,
    behind_send,
    behind_recv,
    sums_send,
    sums_recv,
):
    tiles, subs, side, blk_dev, block, slots, rhs = cfg
    half = blk_dev // 2
    t = lax.axis_index("tile")
    s = lax.axis_index("sub")
    core = lax.rem(t, 2)
    above = lax.rem(s + 1, subs)
    below = lax.rem(s + subs - 1, subs)
    across = lax.rem(s + 2, subs)
    has_behind = t > 0
    has_ahead = t < tiles - 1

    loads = [
        pltpu.make_async_copy(right_hbm, right, in_sem.at[0]),
        pltpu.make_async_copy(order_hbm, order, in_sem.at[1]),
        pltpu.make_async_copy(pairs_hbm, pairs, in_sem.at[2]),
        pltpu.make_async_copy(noise_hbm, noise, in_sem.at[3]),
        pltpu.make_async_copy(diag_hbm, diag, in_sem.at[4]),
    ]
    step = slots // PARTS
    block_loads = [
        pltpu.make_async_copy(
            blocks_hbm.at[pl.ds(i * step, step)],
            blocks.at[pl.ds(i * step, step)],
            blocks_sem.at[i],
        )
        for i in range(PARTS)
    ]
    for copy in loads[:2]:
        copy.start()

    group = core * subs + s
    chip_x = lax.rem(t // 2, side)
    chip_y = t // (2 * side)

    def column_partner(index):
        return (t - core + index // subs, lax.rem(index, subs))

    def x_partner(index):
        return ((chip_y * side + index) * 2 + core, s)

    def y_partner(index):
        return ((index * side + chip_x) * 2 + core, s)

    def plane_partner(index):
        return (index * 2 + core, s)

    stages = (
        (2 * subs, group, column_partner, 0),
        (side, chip_x, x_partner, 2 * subs),
        (side, chip_y, y_partner, 2 * subs + side),
    )
    last_stages = (stages[0], (tiles // 2, t // 2, plane_partner, 2 * subs))

    def stages_of(k):
        return last_stages if k == ITERS - 1 else stages

    barrier = pltpu.get_barrier_semaphore()
    greeted = 0
    for count, mine, partner, unused in stages:
        for j in range(1, count):
            pl.semaphore_signal(
                barrier, inc=1, device_id=partner(lax.rem(mine + j, count)), device_id_type=MESH
            )
            greeted += 1
    far_ahead = (core == 1) & has_ahead
    far_behind = (core == 0) & has_behind

    @pl.when(far_ahead)
    def _():
        pl.semaphore_signal(barrier, inc=1, device_id=(t + 1, s), device_id_type=MESH)

    @pl.when(far_behind)
    def _():
        pl.semaphore_signal(barrier, inc=1, device_id=(t - 1, s), device_id_type=MESH)

    for copy in block_loads[:1]:
        copy.start()
    for copy in loads[2:]:
        copy.start()
    for copy in block_loads[1:]:
        copy.start()

    chunks = right.shape[1] // LANES

    def permute(i, carry):
        at = pl.multiple_of(i * LANES, LANES)
        index = jnp.broadcast_to(order[:, pl.ds(at, LANES)], (rhs, LANES))
        low = lax.bitwise_and(index, LANES - 1)
        high = lax.shift_right_logical(index, 7)
        out = jnp.zeros((rhs, LANES), F32)
        for h in range(chunks):
            picked = jnp.take_along_axis(right[:, h * LANES : (h + 1) * LANES], low, axis=1)
            out = jnp.where(high == h, picked, out)
        base[:, pl.ds(at, LANES)] = out
        return carry

    def put_field(k, values, h):
        for b in range(h * half, (h + 1) * half):
            at = (b - h * half) * block
            field[k, s * blk_dev + b] = values[:, at : at + block].astype(BF16)

    def pieces(k):
        return 2 if k == 0 else 1

    def field_piece(k, row, h):
        length = blk_dev // pieces(k)
        return field.at[k, pl.ds(row * blk_dev + h * length, length)]

    targets = (across, above, below)
    sources = (across, below, above)

    def field_copy(k, row, h, n):
        return pltpu.make_async_remote_copy(
            src_ref=field_piece(k, row, h),
            dst_ref=field_piece(k, row, h),
            send_sem=field_send.at[k, n, h],
            recv_sem=field_recv.at[k, row, h],
            device_id=(t, targets[n]),
            device_id_type=MESH,
        )

    def ahead_copy(k, h):
        length = blk_dev // pieces(k)
        return pltpu.make_async_remote_copy(
            src_ref=field_piece(k, 0, h),
            dst_ref=field_ahead.at[k, pl.ds(h * length, length)],
            send_sem=ahead_send.at[k, h],
            recv_sem=ahead_recv.at[k, h],
            device_id=(t - 1, s),
            device_id_type=MESH,
        )

    def pass_back(k, row, h):
        @pl.when((row == 0) & has_behind)
        def _():
            ahead_copy(k, h).start()

    def start_field(k, h):
        for n in range(3):
            field_copy(k, s, h, n).start()
        pass_back(k, s, h)

    def finish_field(k):
        for h in range(pieces(k)):
            for n in (1, 2, 0):
                field_copy(k, sources[n], h, n).wait_recv()
                pass_back(k, sources[n], h)

    def finish_ahead(k):
        @pl.when(has_ahead)
        def _():
            for h in range(pieces(k)):
                ahead_copy(k, h).wait_recv()

        for b in range(blk_dev):
            field[k, subs * blk_dev + b] = field_ahead[k, b]

    def drain_field(k):
        for h in range(pieces(k)):
            for n in range(3):
                field_copy(k, s, h, n).wait_send()

        @pl.when(has_behind)
        def _():
            for h in range(pieces(k)):
                ahead_copy(k, h).wait_send()

    def sums_copy(k, stage, j, incoming):
        count, mine, partner, offset = stages_of(k)[stage]
        other = lax.rem(mine + j, count)
        at = offset + (other if incoming else mine)
        return pltpu.make_async_remote_copy(
            src_ref=sums.at[k, at],
            dst_ref=sums.at[k, at],
            send_sem=sums_send.at[k, offset + j],
            recv_sem=sums_recv.at[k, at],
            device_id=partner(other),
            device_id_type=MESH,
        )

    def sums_start(k, stage, values):
        count, mine, partner, offset = stages_of(k)[stage]
        sums[k, offset + mine] = values
        for j in range(1, count):
            sums_copy(k, stage, j, False).start()

    def sums_finish(k, stage):
        count, mine, partner, offset = stages_of(k)[stage]
        for j in range(1, count):
            sums_copy(k, stage, j, True).wait_recv()
        total = sums[k, offset]
        for j in range(1, count):
            total = total + sums[k, offset + j]
        return total

    def sums_drain(k):
        for stage, (count, *unused) in enumerate(stages_of(k)):
            for j in range(1, count):
                sums_copy(k, stage, j, False).wait_send()

    def fold(values):
        parts = [values[:, i : i + LANES] for i in range(0, values.shape[1], LANES)]
        while len(parts) > 1:
            parts = [a + b for a, b in zip(parts[::2], parts[1::2])]
        return parts[0]

    spot = lax.broadcasted_iota(jnp.int32, (rhs, LANES), 1) - lax.broadcasted_iota(
        jnp.int32, (rhs, LANES), 0
    )

    def pack(*folded):
        out = jnp.zeros((rhs, LANES), F32)
        for n, values in enumerate(folded):
            column = jnp.sum(values, axis=1, keepdims=True)
            out = jnp.where(spot == n * rhs, column, out)
        return jnp.sum(out, axis=0, keepdims=True)

    def unpack(total, n):
        wide = jnp.broadcast_to(total, (rhs, LANES))
        return jnp.sum(jnp.where(spot == n * rhs, wide, 0.0), axis=1, keepdims=True)

    first = t * (subs * blk_dev)
    middle = slots // 2
    tile_blocks = subs * blk_dev

    def build_table():
        shape = (8, LANES)
        sub_id = lax.broadcasted_iota(jnp.int32, shape, 0)
        lane_id = lax.broadcasted_iota(jnp.int32, shape, 1)
        ids = sub_id * LANES + lane_id

        def add_slot(i, carry):
            found, listed, low, high = carry
            for u in range(8):
                p = i * 8 + u
                row = pairs[0, p]
                col = pairs[1, p]
                live = row >= 0
                reach = jnp.where(col - first >= tile_blocks, 1, 0)
                place = jnp.where(reach == 1, low, high)
                low = low + reach
                high = high - (1 - reach)
                apart = col - row
                kind = jnp.where(apart == 1, 0, apart - (blk_dev - 2))
                key_col = jnp.where(live, (col - first) * 4 + kind, -1)
                key_row = jnp.where(live, (row - first) * 4 + kind + 4 * LANES, -1)
                found = jnp.where((ids == key_col) | (ids == key_row), place + 1, found)
                entry = jnp.where(
                    sub_id == 0,
                    p,
                    jnp.where(
                        sub_id == 1, jnp.maximum(row - first, 0), jnp.maximum(col - first, 0)
                    ),
                )
                listed = jnp.where(lane_id == place, entry, listed)
            return found, listed, low, high

        zeros = jnp.zeros(shape, jnp.int32)
        found, listed, unused_low, unused_high = lax.fori_loop(
            0, slots // 8, add_slot, (zeros, zeros, jnp.int32(0), jnp.int32(slots - 1))
        )
        table_vec[0:8] = found
        table_vec[8:16] = listed
        move = pltpu.make_async_copy(table_vec, table, table_sem)
        move.start()
        move.wait()
        col_out[0] = jnp.zeros((rhs, block), F32)
        row_out[0] = jnp.zeros((rhs, block), F32)

    def diag_products(k):
        def body(i, carry):
            for u in range(8):
                b = i * 8 + u
                at = pl.multiple_of(b * block, block)
                own_part[:, pl.ds(at, block)] = jnp.dot(
                    field[k, s * blk_dev + b], diag[b], preferred_element_type=F32
                )
            return carry

        lax.fori_loop(0, blk_dev // 8, body, 0)

    def listed_sum(out, line, q, kinds):
        at = q * 4
        row = line + at // LANES
        lane = lax.rem(at, LANES)
        parts = [out[table[row, lane + n]] for n in kinds]
        while len(parts) > 1:
            paired = [x + y for x, y in zip(parts[::2], parts[1::2])]
            parts = paired + parts[len(paired) * 2 :]
        return parts[0]

    across_rows = (((1,), (0,)), ((), ()))
    across_cols = (((1,), (1,)), ((), ()))

    def turn(p):
        turned[p] = blocks[table[8, p]].T

    def col_products(k, low, also=()):
        total = jnp.zeros((rhs, block), F32)
        for u in range(middle):
            p = low + u
            out = lax.dot_general(
                field[k, table[9, p]],
                blocks[table[8, p]],
                across_rows,
                preferred_element_type=F32,
            )
            col_out[1 + p] = out
            if k == ITERS - 1 and low > 0:
                total = total + out * field[k, table[10, p]].astype(F32)
            if u % 2 == 0 and u // 2 < len(also):
                turn(also[u // 2])
        return total

    def row_products(k, low, is_turned, line, also=()):
        share = tile_blocks // 2
        for u in range(middle):
            p = low + u
            if is_turned(p):
                row_out[1 + p] = lax.dot_general(
                    field[k, table[10, p]],
                    turned[p],
                    across_rows,
                    preferred_element_type=F32,
                )
            else:
                row_out[1 + p] = lax.dot_general(
                    field[k, table[10, p]],
                    blocks[table[8, p]],
                    across_cols,
                    preferred_element_type=F32,
                )
            if u < share:
                q = line * share + u
                half_sums[q] = listed_sum(col_out, 0, q, range(4))
            if u % 2 == 0 and u // 2 < len(also):
                turn(also[u // 2])

    def quadratic(k, total):
        def body(i, total):
            for u in range(8):
                p = i * 8 + u
                total = total + col_out[1 + p] * field[k, table[10, p]].astype(F32)
            return total

        return fold(lax.fori_loop(0, middle // 8, body, total))

    def partial_sum(row, b):
        q = row * blk_dev + b
        return half_sums[q] + listed_sum(row_out, 4, q, range(4))

    def remote(src, dst, send, recv, target):
        return pltpu.make_async_remote_copy(
            src_ref=src,
            dst_ref=dst,
            send_sem=send,
            recv_sem=recv,
            device_id=target,
            device_id_type=MESH,
        )

    def part_copy(k, n):
        return remote(
            parts_out.at[k, n], parts_in.at[k, n], part_send.at[k, n], part_recv.at[k, n], (t, targets[n])
        )

    def behind_copy(k):
        return remote(
            to_ahead.at[k],
            from_behind.at[k],
            behind_send.at[k],
            behind_recv.at[k],
            (t + 1, s),
        )

    def send_ahead(k):
        @pl.when(has_ahead)
        def _():
            def body(i, carry):
                for u in range(8):
                    b = i * 8 + u
                    q = subs * blk_dev + b
                    to_ahead[k, b] = listed_sum(col_out, 0, q, (1, 2, 3)).astype(BF16)
                return carry

            lax.fori_loop(0, blk_dev // 8, body, 0)
            behind_copy(k).start()

    def send_products(k):
        @pl.when(has_behind)
        def _():
            behind_copy(k).wait_recv()

        for b in range(blk_dev):
            half_sums[b] = half_sums[b] + from_behind[k, b].astype(F32)

        for n in range(3):

            def body(i, carry):
                for u in range(8):
                    b = i * 8 + u
                    parts_out[k, n, b] = partial_sum(targets[n], b).astype(BF16)
                return carry

            lax.fori_loop(0, blk_dev // 8, body, 0)
            part_copy(k, n).start()

    def own_products(k):
        def body(i, carry):
            for u in range(4):
                b = i * 4 + u
                at = pl.ds(pl.multiple_of(b * block, block), block)
                own_part[:, at] = own_part[:, at] + partial_sum(s, b)
            return carry

        lax.fori_loop(0, blk_dev // 4, body, 0)

    def take_products(k, vector, out):
        for n in (1, 2, 0):
            part_copy(k, n).wait_recv()
        for b in range(blk_dev):
            at = slice(b * block, (b + 1) * block)
            total = parts_in[k, 0, b].astype(F32) + parts_in[k, 1, b].astype(F32)
            total = total + parts_in[k, 2, b].astype(F32)
            out[:, at] = total + (own_part[:, at] + noise[:, at] * vector[:, at])

    def drain_products(k):
        for n in range(3):
            part_copy(k, n).wait_send()

        @pl.when(has_ahead)
        def _():
            behind_copy(k).wait_send()


    loads[0].wait()
    loads[1].wait()
    with scope("permute0"):
        lax.fori_loop(0, chunks // 2, permute, 0)
        put_field(0, base[:, 0 : half * block], 0)
    with scope("barrier"):
        pl.semaphore_wait(barrier, greeted + jnp.where(far_ahead | far_behind, 1, 0))
    start_field(0, 0)
    with scope("permute1"):
        lax.fori_loop(chunks // 2, chunks, permute, 0)
        put_field(0, base[:, half * block :], 1)
    start_field(0, 1)

    @pl.when(jnp.logical_not(has_ahead))
    def _():
        for k in range(ITERS):
            field_ahead[k] = jnp.zeros((blk_dev, rhs, block), BF16)

    @pl.when(jnp.logical_not(has_behind))
    def _():
        for k in range(ITERS):
            from_behind[k] = jnp.zeros((blk_dev, rhs, block), BF16)

    loads[2].wait()
    with scope("table"):
        build_table()
    loads[4].wait()
    with scope("diag0"):
        diag_products(0)
    with scope("finish0"):
        finish_field(0)
    for copy in block_loads:
        copy.wait()
    with scope("cols0"):
        quarter = middle // 2
        col_products(0, 0, range(middle, middle + quarter))
        send_ahead(0)
        col_products(0, middle, range(middle + quarter, slots))
    with scope("rows0"):
        row_products(0, middle, lambda p: True, 0, range(quarter))
        finish_ahead(0)
        row_products(0, 0, lambda p: p < quarter, 1, range(quarter, middle))
    with scope("send0"):
        send_products(0)
    with scope("own0"):
        own_products(0)
    loads[3].wait()
    with scope("take0"):
        take_products(0, base, image)

    with scope("sums0"):
        b_now = base[...]
        q_now = image[...]
        sums_start(0, 0, pack(fold(b_now * b_now), fold(b_now * q_now), fold(q_now * q_now)))
    with scope("start1"):
        put_field(1, image[:, 0 : half * block], 0)
        put_field(1, image[:, half * block :], 1)
        start_field(1, 0)
    with scope("diag1"):
        diag_products(1)
    with scope("finish1"):
        finish_field(1)
    with scope("sums0b"):
        sums_start(0, 1, sums_finish(0, 0))
    with scope("cols1"):
        col_products(1, 0)
        send_ahead(1)
        col_products(1, middle)
    with scope("rows1"):
        row_products(1, middle, lambda p: True, 0)
    with scope("sums0c"):
        sums_start(0, 2, sums_finish(0, 1))
    with scope("rows1b"):
        finish_ahead(1)
        row_products(1, 0, lambda p: True, 1)
    with scope("send1"):
        send_products(1)
    with scope("own1"):
        own_products(1)
    with scope("sums0d"):
        total = sums_finish(0, 2)
        norm0 = unpack(total, 0)
        curve0 = unpack(total, 1)
        square0 = unpack(total, 2)
        step0 = norm0 / curve0
        rate0 = curve0 / norm0
        norm1 = norm0 - 2.0 * step0 * curve0 + step0 * step0 * square0
        mix0 = norm1 / norm0
        resid[...] = base[...] - step0 * image[...]
        direct[...] = resid[...] + mix0 * base[...]
    with scope("take1"):
        take_products(1, image, twice)

    with scope("start2"):
        resid_image[...] = image[...] - step0 * twice[...]
        image_next[...] = resid_image[...] + mix0 * image[...]
        image[...] = image_next[...] - rate0 * resid[...]
    with scope("sums1"):
        q_now = image_next[...]
        sums_start(
            1,
            0,
            pack(
                fold(direct[...] * q_now),
                fold(resid[...] * q_now),
                fold(q_now * q_now),
                fold(resid[...] * resid_image[...]),
                fold(q_now * resid_image[...]),
            ),
        )
    with scope("start2b"):
        put_field(2, image[:, 0 : half * block], 0)
        put_field(2, image[:, half * block :], 1)
        start_field(2, 0)
    with scope("diag2"):
        diag_products(2)
        w_now = image[...]
        local = fold(w_now * (own_part[...] + noise[...] * w_now))
    with scope("finish2"):
        finish_field(2)
    with scope("sums1b"):
        sums_start(1, 1, sums_finish(1, 0))
    with scope("cols2"):
        col_products(2, 0)
        send_ahead(2)
        total = col_products(2, middle)
        finish_ahead(2)
    with scope("sums2"):
        sums_start(2, 0, pack(local + 2.0 * quadratic(2, total)))
    with scope("rows2"):
        row_products(2, 0, lambda p: True, 0)
    with scope("sums1c"):
        sums_start(1, 2, sums_finish(1, 1))
    with scope("rows2b"):
        row_products(2, middle, lambda p: True, 1)
    with scope("sums2b"):
        sums_start(2, 1, sums_finish(2, 0))
    with scope("send2"):
        send_products(2)
    with scope("own2"):
        own_products(2)
    with scope("sums2d"):
        total = sums_finish(1, 2)
        curve1 = unpack(total, 0)
        cross1 = unpack(total, 1)
        square1 = unpack(total, 2)
        inner_rr = unpack(total, 3)
        inner_qr = unpack(total, 4)
        step1 = norm1 / curve1
        norm2 = norm1 - 2.0 * step1 * cross1 + step1 * step1 * square1
        mix1 = norm2 / norm1
        keep = 1.0 - step1 * rate0
        inner_ww = unpack(sums_finish(2, 1), 0)
        inner_wr = inner_qr - rate0 * inner_rr
        inner_wq = square1 - rate0 * cross1
        curve2 = (
            step1 * step1 * inner_ww
            + keep * keep * inner_rr
            + mix1 * mix1 * curve1
            - 2.0 * keep * step1 * inner_wr
            + 2.0 * keep * mix1 * cross1
            - 2.0 * step1 * mix1 * inner_wq
        )
        step2 = norm2 / curve2
        r_now = resid[...] - step1 * image_next[...]
        d_now = r_now + mix1 * direct[...]
        sol_ref[...] = step0 * base[...] + step1 * direct[...] + step2 * d_now
        resid[...] = r_now - step2 * (keep * resid_image[...] + mix1 * image_next[...])
    with scope("take2"):
        take_products(2, image, twice)
        res_ref[...] = resid[...] + (step2 * step1) * twice[...]

    with scope("drain"):
        for k in range(ITERS):
            drain_field(k)
            drain_products(k)
            sums_drain(k)


def solution(mesh):
    tiles, subs = mesh.shape["tile"], mesh.shape["sub"]
    side = math.isqrt(tiles // 2)

    def on_device(right_side, point_order, noise_var, block_pairs, pair_blocks, diag_blocks):
        rhs, points = right_side.shape
        slots, block = pair_blocks.shape[:2]
        blk_dev = diag_blocks.shape[0]
        cfg = (tiles, subs, side, blk_dev, block, slots, rhs)
        members = 2 * subs + max(2 * side, tiles // 2)
        vec = pltpu.VMEM((rhs, points), F32)
        row = pltpu.VMEM((ITERS, blk_dev, rhs, block), BF16)
        dma = pltpu.SemaphoreType.DMA
        return pl.pallas_call(
            functools.partial(kernel, cfg),
            out_shape=(jax.ShapeDtypeStruct((rhs, points), F32),) * 2,
            in_specs=[pl.BlockSpec(memory_space=pltpu.MemorySpace.HBM)] * 6,
            out_specs=(pl.BlockSpec(memory_space=pltpu.VMEM),) * 2,
            scratch_shapes=[
                vec,
                pltpu.VMEM((1, points), jnp.int32),
                pltpu.VMEM((1, points), F32),
                pltpu.SMEM((2, slots), jnp.int32),
                pltpu.VMEM((slots, block, block), BF16),
                pltpu.VMEM((blk_dev, block, block), BF16),
                vec,
                vec,
                vec,
                vec,
                vec,
                vec,
                vec,
                vec,
                pltpu.VMEM((ITERS, (subs + 1) * blk_dev, rhs, block), BF16),
                row,
                pltpu.VMEM((1 + slots, rhs, block), F32),
                pltpu.VMEM((1 + slots, rhs, block), F32),
                pltpu.VMEM((subs * blk_dev, rhs, block), F32),
                pltpu.VMEM((slots, block, block), BF16),
                pltpu.VMEM((ITERS, 3, blk_dev, rhs, block), BF16),
                pltpu.VMEM((ITERS, 3, blk_dev, rhs, block), BF16),
                row,
                row,
                pltpu.VMEM((16, LANES), jnp.int32),
                pltpu.SMEM((16, LANES), jnp.int32),
                pltpu.VMEM((ITERS, members, 1, LANES), F32),
                dma((5,)),
                dma((PARTS,)),
                dma,
                dma((ITERS, 3, 2)),
                dma((ITERS, subs, 2)),
                dma((ITERS, 2)),
                dma((ITERS, 2)),
                dma((ITERS, 3)),
                dma((ITERS, 3)),
                dma((ITERS,)),
                dma((ITERS,)),
                dma((ITERS, members)),
                dma((ITERS, members)),
            ],
            compiler_params=pltpu.CompilerParams(
                collective_id=0, has_side_effects=True, vmem_limit_bytes=50 << 20
            ),
            name="block_pair_solve",
        )(
            *(
                pltpu.with_memory_space_constraint(value, pltpu.MemorySpace.HBM)
                for value in (
                    right_side,
                    point_order,
                    noise_var.reshape(1, -1),
                    block_pairs.T,
                    pair_blocks,
                    diag_blocks,
                )
            )
        )

    both = ("tile", "sub")
    return jax.shard_map(
        on_device,
        mesh=mesh,
        in_specs=(
            P(None, both),
            P(both, None),
            P(both),
            P(both, None),
            P(both, None, None),
            P(both, None, None),
        ),
        out_specs=(P(None, both), P(None, both)),
        check_vma=False,
    )
```

```python
import functools
import math

import jax
import jax.numpy as jnp
from jax import lax
from jax.experimental import pallas as pl
from jax.experimental.pallas import tpu as pltpu
from jax.sharding import PartitionSpec as P

ITERS = 3
PARTS = 6
LANES = 128
F32 = jnp.float32
BF16 = jnp.bfloat16
MESH = pl.DeviceIdType.MESH


def scope(name):
    return jax.named_scope(name)


def kernel(
    cfg,
    right_hbm,
    order_hbm,
    noise_hbm,
    pairs_hbm,
    blocks_hbm,
    diag_hbm,
    sol_ref,
    res_ref,
    right,
    order,
    noise,
    pairs,
    blocks,
    diag,
    base,
    image,
    twice,
    resid,
    direct,
    image_next,
    resid_image,
    own_part,
    field,
    field_ahead,
    col_out,
    row_out,
    half_sums,
    turned,
    parts_out,
    parts_in,
    to_ahead,
    from_behind,
    table_vec,
    table,
    sums,
    in_sem,
    blocks_sem,
    table_sem,
    field_send,
    field_recv,
    ahead_send,
    ahead_recv,
    part_send,
    part_recv,
    behind_send,
    behind_recv,
    sums_send,
    sums_recv,
):
    tiles, subs, side, blk_dev, block, slots, rhs = cfg
    t = lax.axis_index("tile")
    s = lax.axis_index("sub")
    core = lax.rem(t, 2)
    above = lax.rem(s + 1, subs)
    below = lax.rem(s + subs - 1, subs)
    across = lax.rem(s + 2, subs)
    has_behind = t > 0
    has_ahead = t < tiles - 1

    loads = [
        pltpu.make_async_copy(right_hbm, right, in_sem.at[0]),
        pltpu.make_async_copy(order_hbm, order, in_sem.at[1]),
        pltpu.make_async_copy(pairs_hbm, pairs, in_sem.at[2]),
        pltpu.make_async_copy(noise_hbm, noise, in_sem.at[3]),
        pltpu.make_async_copy(diag_hbm, diag, in_sem.at[4]),
    ]
    step = slots // PARTS
    block_loads = [
        pltpu.make_async_copy(
            blocks_hbm.at[pl.ds(i * step, step)],
            blocks.at[pl.ds(i * step, step)],
            blocks_sem,
        )
        for i in range(PARTS)
    ]
    for copy in loads[:2]:
        copy.start()

    group = core * subs + s
    chip_x = lax.rem(t // 2, side)
    chip_y = t // (2 * side)

    def column_partner(index):
        return (t - core + index // subs, lax.rem(index, subs))

    def x_partner(index):
        return ((chip_y * side + index) * 2 + core, s)

    def y_partner(index):
        return ((index * side + chip_x) * 2 + core, s)

    def plane_partner(index):
        return (index * 2 + core, s)

    stages = (
        (2 * subs, group, column_partner, 0),
        (side, chip_x, x_partner, 2 * subs),
        (side, chip_y, y_partner, 2 * subs + side),
    )
    last_stages = (stages[0], (tiles // 2, t // 2, plane_partner, 2 * subs))

    def stages_of(k):
        return last_stages if k == ITERS - 1 else stages

    barrier = pltpu.get_barrier_semaphore()
    greeted = 0
    for count, mine, partner, unused in stages:
        for j in range(1, count):
            pl.semaphore_signal(
                barrier, inc=1, device_id=partner(lax.rem(mine + j, count)), device_id_type=MESH
            )
            greeted += 1
    far_ahead = (core == 1) & has_ahead
    far_behind = (core == 0) & has_behind

    @pl.when(far_ahead)
    def _():
        pl.semaphore_signal(barrier, inc=1, device_id=(t + 1, s), device_id_type=MESH)

        @pl.when(s > 0)
        def _():
            pl.semaphore_signal(barrier, inc=1, device_id=(t + 1, 0), device_id_type=MESH)

    @pl.when(far_behind)
    def _():
        pl.semaphore_signal(barrier, inc=1, device_id=(t - 1, s), device_id_type=MESH)

        @pl.when(s == 0)
        def _():
            for j in range(1, subs):
                pl.semaphore_signal(barrier, inc=1, device_id=(t - 1, j), device_id_type=MESH)

    for copy in block_loads[:1]:
        copy.start()
    for copy in loads[2:]:
        copy.start()
    for copy in block_loads[1:]:
        copy.start()

    chunks = right.shape[1] // LANES

    def permute(i, carry):
        for u in range(4):
            chunk = (i % (chunks // 8) * 4 + u) * 2 + i // (chunks // 8)
            at = pl.multiple_of(chunk * LANES, LANES)
            index = jnp.broadcast_to(order[:, pl.ds(at, LANES)], (rhs, LANES))
            low = lax.bitwise_and(index, LANES - 1)
            high = lax.shift_right_logical(index, 7)
            out = jnp.zeros((rhs, LANES), F32)
            for h in range(chunks):
                picked = jnp.take_along_axis(right[:, h * LANES : (h + 1) * LANES], low, axis=1)
                out = jnp.where(high == h, picked, out)
            base[:, pl.ds(at, LANES)] = out
        return carry

    def put_field(k, values, h):
        for b in range(blk_dev):
            at = b * block + h * LANES
            field[k, h, s * blk_dev + b] = values[:, at : at + LANES].astype(BF16)

    def whole(k, q):
        return jnp.concatenate([field[k, 0, q], field[k, 1, q]], axis=1)

    def remote(src, dst, send, recv, target):
        return pltpu.make_async_remote_copy(
            src_ref=src,
            dst_ref=dst,
            send_sem=send,
            recv_sem=recv,
            device_id=target,
            device_id_type=MESH,
        )

    targets = (across, above, below)
    sources = (across, below, above)

    def field_copy(k, row, h, n):
        part = field.at[k, h, pl.ds(row * blk_dev, blk_dev)]
        return remote(part, part, field_send.at[k], field_recv.at[k, h, n], (t, targets[n]))

    def ahead_copy(k, h, to):
        return remote(
            field.at[k, h, pl.ds(0, blk_dev)],
            field_ahead.at[k, h],
            ahead_send.at[k],
            ahead_recv.at[k],
            (t - 1, to),
        )

    def ahead_waits(k):
        both = field_ahead.at[k]
        return remote(both, both, ahead_send.at[k], ahead_recv.at[k], (t, above))

    def pass_back(k, row, h):
        @pl.when((row == 0) & (core == 1))
        def _():
            ahead_copy(k, h, s).start()

    def send_behind(k):
        @pl.when((s == 0) & far_behind)
        def _():
            for h in range(2):
                for j in (2, 1, 3, 0):
                    ahead_copy(k, h, j).start()

    def start_field(k, h):
        for n in range(3):
            field_copy(k, s, h, n).start()
        pass_back(k, s, h)

    def finish_field(k):
        for n in (1, 2, 0):
            for h in range(2):
                field_copy(k, sources[n], h, n).wait_recv()
                pass_back(k, sources[n], h)

    def finish_ahead(k):
        @pl.when(has_ahead)
        def _():
            ahead_waits(k).wait_recv()

        for h in range(2):
            for b in range(blk_dev):
                field[k, h, subs * blk_dev + b] = field_ahead[k, h, b]

    def drain_field(k):
        sent = parts_out.at[k]
        remote(sent, sent, field_send.at[k], field_recv.at[k, 0, 0], (t, above)).wait_send()

        @pl.when(core == 1)
        def _():
            ahead_waits(k).wait_send()

        @pl.when((s == 0) & far_behind)
        def _():
            sent = field.at[k, :, pl.ds(0, subs * blk_dev)]
            remote(sent, sent, ahead_send.at[k], ahead_recv.at[k], (t, above)).wait_send()

    def sums_start(k, stage, values):
        count, mine, partner, offset = stages_of(k)[stage]
        sums[k, offset + mine] = values
        own = sums.at[k, offset + mine]
        for j in range(1, count):
            remote(
                own,
                own,
                sums_send.at[k, stage],
                sums_recv.at[k, stage],
                partner(lax.rem(mine + j, count)),
            ).start()

    def sums_waits(k, stage):
        count, mine, partner, offset = stages_of(k)[stage]
        others = sums.at[k, pl.ds(offset, count - 1)]
        return remote(
            others, others, sums_send.at[k, stage], sums_recv.at[k, stage], (t, above)
        )

    def sums_finish(k, stage):
        count, mine, partner, offset = stages_of(k)[stage]
        sums_waits(k, stage).wait_recv()
        total = sums[k, offset]
        for j in range(1, count):
            total = total + sums[k, offset + j]
        return total

    def sums_drain(k):
        for stage in range(len(stages_of(k))):
            sums_waits(k, stage).wait_send()

    def fold(values):
        parts = [values[:, i : i + LANES] for i in range(0, values.shape[1], LANES)]
        while len(parts) > 1:
            parts = [a + b for a, b in zip(parts[::2], parts[1::2])]
        return parts[0]

    spot = lax.broadcasted_iota(jnp.int32, (rhs, LANES), 1) - lax.broadcasted_iota(
        jnp.int32, (rhs, LANES), 0
    )

    def pack(*folded):
        out = jnp.zeros((rhs, LANES), F32)
        for n, values in enumerate(folded):
            column = jnp.sum(values, axis=1, keepdims=True)
            out = jnp.where(spot == n * rhs, column, out)
        return jnp.sum(out, axis=0, keepdims=True)

    def unpack(total, n):
        wide = jnp.broadcast_to(total, (rhs, LANES))
        return jnp.sum(jnp.where(spot == n * rhs, wide, 0.0), axis=1, keepdims=True)

    first = t * (subs * blk_dev)
    middle = slots // 2
    tile_blocks = subs * blk_dev

    def build_table():
        shape = (8, LANES)
        sub_id = lax.broadcasted_iota(jnp.int32, shape, 0)
        lane_id = lax.broadcasted_iota(jnp.int32, shape, 1)
        ids = sub_id * LANES + lane_id

        def add_slot(i, carry):
            found, listed, low, high = carry
            for u in range(8):
                p = i * 8 + u
                row = pairs[0, p]
                col = pairs[1, p]
                live = row >= 0
                reach = jnp.where(col - first >= tile_blocks, 1, 0)
                place = jnp.where(reach == 1, low, high)
                low = low + reach
                high = high - (1 - reach)
                apart = col - row
                kind = jnp.where(apart == 1, 0, apart - (blk_dev - 2))
                key_col = jnp.where(live, (col - first) * 4 + kind, -1)
                key_row = jnp.where(live, (row - first) * 4 + kind + 4 * LANES, -1)
                found = jnp.where((ids == key_col) | (ids == key_row), place + 1, found)
                entry = jnp.where(
                    sub_id == 0,
                    p,
                    jnp.where(
                        sub_id == 1, jnp.maximum(row - first, 0), jnp.maximum(col - first, 0)
                    ),
                )
                listed = jnp.where(lane_id == place, entry, listed)
            return found, listed, low, high

        zeros = jnp.zeros(shape, jnp.int32)
        found, listed, unused_low, unused_high = lax.fori_loop(
            0, slots // 8, add_slot, (zeros, zeros, jnp.int32(0), jnp.int32(slots - 1))
        )
        table_vec[0:8] = found
        table_vec[8:16] = listed
        move = pltpu.make_async_copy(table_vec, table, table_sem)
        move.start()
        move.wait()
        col_out[0] = jnp.zeros((rhs, block), F32)
        row_out[0] = jnp.zeros((rhs, block), F32)

    def diag_products(k):
        def body(i, carry):
            for u in range(8):
                b = i * 8 + u
                at = pl.multiple_of(b * block, block)
                own_part[:, pl.ds(at, block)] = jnp.dot(
                    whole(k, s * blk_dev + b), diag[b], preferred_element_type=F32
                )
            return carry

        lax.fori_loop(0, blk_dev // 8, body, 0)

    def listed_sum(out, line, q, kinds):
        at = q * 4
        row = line + at // LANES
        lane = lax.rem(at, LANES)
        parts = [out[table[row, lane + n]] for n in kinds]
        while len(parts) > 1:
            paired = [x + y for x, y in zip(parts[::2], parts[1::2])]
            parts = paired + parts[len(paired) * 2 :]
        return parts[0]

    across_rows = (((1,), (0,)), ((), ()))
    across_cols = (((1,), (1,)), ((), ()))

    def turn(p):
        turned[p] = blocks[table[8, p]].T

    def dot(left, right_block, dims):
        return lax.dot_general(left, right_block, dims, preferred_element_type=F32)

    def col_products(k, low, also=()):
        total = jnp.zeros((rhs, block), F32)
        for u in range(middle):
            p = low + u
            out = dot(whole(k, table[9, p]), blocks[table[8, p]], across_rows)
            col_out[1 + p] = out
            if k == ITERS - 1 and low > 0:
                total = total + out * whole(k, table[10, p]).astype(F32)
            if u % 2 == 0 and u // 2 < len(also):
                turn(also[u // 2])
        return total

    def row_products(k, low, is_turned, line, also=()):
        share = tile_blocks // 2
        for u in range(middle):
            p = low + u
            left = whole(k, table[10, p])
            if is_turned(p):
                row_out[1 + p] = dot(left, turned[p], across_rows)
            else:
                row_out[1 + p] = dot(left, blocks[table[8, p]], across_cols)
            if u < share:
                q = line * share + u
                half_sums[q] = listed_sum(col_out, 0, q, range(4))
            if u % 2 == 0 and u // 2 < len(also):
                turn(also[u // 2])

    def quadratic(k, total):
        def body(i, total):
            for u in range(8):
                p = i * 8 + u
                total = total + col_out[1 + p] * whole(k, table[10, p]).astype(F32)
            return total

        return fold(lax.fori_loop(0, middle // 8, body, total))

    def partial_sum(row, b):
        q = row * blk_dev + b
        return half_sums[q] + listed_sum(row_out, 4, q, range(4))

    def part_copy(k, n):
        return remote(
            parts_out.at[k, n], parts_in.at[k, n], part_send.at[k], part_recv.at[k], (t, targets[n])
        )

    def part_waits(k):
        return remote(
            parts_out.at[k], parts_in.at[k], part_send.at[k], part_recv.at[k], (t, above)
        )

    def behind_copy(k):
        return remote(
            to_ahead.at[k],
            from_behind.at[k],
            behind_send.at[k],
            behind_recv.at[k],
            (t + 1, s),
        )

    def send_ahead(k):
        @pl.when(has_ahead)
        def _():
            def body(i, carry):
                for u in range(8):
                    b = i * 8 + u
                    q = subs * blk_dev + b
                    to_ahead[k, b] = listed_sum(col_out, 0, q, (1, 2, 3)).astype(BF16)
                return carry

            lax.fori_loop(0, blk_dev // 8, body, 0)
            behind_copy(k).start()

    def send_products(k):
        @pl.when(has_behind)
        def _():
            behind_copy(k).wait_recv()

        for b in range(blk_dev):
            half_sums[b] = half_sums[b] + from_behind[k, b].astype(F32)

        for n in range(3):

            def body(i, carry):
                for u in range(8):
                    b = i * 8 + u
                    parts_out[k, n, b] = partial_sum(targets[n], b).astype(BF16)
                return carry

            lax.fori_loop(0, blk_dev // 8, body, 0)
            part_copy(k, n).start()

    def own_products(k):
        def body(i, carry):
            for u in range(4):
                b = i * 4 + u
                at = pl.ds(pl.multiple_of(b * block, block), block)
                own_part[:, at] = own_part[:, at] + partial_sum(s, b)
            return carry

        lax.fori_loop(0, blk_dev // 4, body, 0)

    def take_products(k, vector, out):
        part_waits(k).wait_recv()
        for b in range(blk_dev):
            at = slice(b * block, (b + 1) * block)
            total = parts_in[k, 0, b].astype(F32) + parts_in[k, 1, b].astype(F32)
            total = total + parts_in[k, 2, b].astype(F32)
            out[:, at] = total + (own_part[:, at] + noise[:, at] * vector[:, at])

    def drain_products(k):
        part_waits(k).wait_send()

        @pl.when(has_ahead)
        def _():
            behind_copy(k).wait_send()


    loads[0].wait()
    loads[1].wait()
    with scope("permute0"):
        lax.fori_loop(0, chunks // 8, permute, 0)
        put_field(0, base[...], 0)
    with scope("barrier"):
        pl.semaphore_wait(barrier, greeted
            + jnp.where(far_ahead | far_behind, 1, 0)
            + jnp.where(far_ahead & (s > 0), 1, 0)
            + jnp.where(far_behind & (s == 0), subs - 1, 0))
    start_field(0, 0)
    with scope("permute1"):
        lax.fori_loop(chunks // 8, chunks // 4, permute, 0)
        put_field(0, base[...], 1)
    start_field(0, 1)
    send_behind(0)

    @pl.when(jnp.logical_not(has_ahead))
    def _():
        for k in range(ITERS):
            field_ahead[k] = jnp.zeros((2, blk_dev, rhs, LANES), BF16)

    @pl.when(jnp.logical_not(has_behind))
    def _():
        for k in range(ITERS):
            from_behind[k] = jnp.zeros((blk_dev, rhs, block), BF16)

    loads[2].wait()
    with scope("table"):
        build_table()
    loads[4].wait()
    with scope("diag0"):
        diag_products(0)
    pltpu.make_async_copy(blocks_hbm, blocks, blocks_sem).wait()
    with scope("finish0"):
        finish_field(0)
    with scope("cols0"):
        quarter = middle // 2
        col_products(0, 0, range(middle, middle + quarter))
        send_ahead(0)
        col_products(0, middle, range(middle + quarter, slots))
    with scope("rows0"):
        row_products(0, middle, lambda p: True, 0, range(quarter))
        finish_ahead(0)
        row_products(0, 0, lambda p: p < quarter, 1, range(quarter, middle))
    with scope("send0"):
        send_products(0)
    with scope("own0"):
        own_products(0)
    loads[3].wait()
    with scope("take0"):
        take_products(0, base, image)

    with scope("sums0"):
        b_now = base[...]
        q_now = image[...]
        sums_start(0, 0, pack(fold(b_now * b_now), fold(b_now * q_now), fold(q_now * q_now)))
    with scope("start1"):
        put_field(1, image[...], 0)
        start_field(1, 0)
        put_field(1, image[...], 1)
        start_field(1, 1)
        send_behind(1)
    with scope("diag1"):
        diag_products(1)
    with scope("finish1"):
        finish_field(1)
    with scope("sums0b"):
        sums_start(0, 1, sums_finish(0, 0))
    with scope("cols1"):
        col_products(1, 0)
        send_ahead(1)
        col_products(1, middle)
    with scope("rows1"):
        row_products(1, middle, lambda p: True, 0)
    with scope("rows1b"):
        finish_ahead(1)
        row_products(1, 0, lambda p: True, 1)
    with scope("send1"):
        send_products(1)
    with scope("sums0c"):
        sums_start(0, 2, sums_finish(0, 1))
    with scope("own1"):
        own_products(1)
    with scope("sums0d"):
        total = sums_finish(0, 2)
        norm0 = unpack(total, 0)
        curve0 = unpack(total, 1)
        square0 = unpack(total, 2)
        step0 = norm0 / curve0
        rate0 = curve0 / norm0
        norm1 = norm0 - 2.0 * step0 * curve0 + step0 * step0 * square0
        mix0 = norm1 / norm0
        resid[...] = base[...] - step0 * image[...]
        direct[...] = resid[...] + mix0 * base[...]
    with scope("take1"):
        take_products(1, image, twice)

    with scope("start2"):
        resid_image[...] = image[...] - step0 * twice[...]
        image_next[...] = resid_image[...] + mix0 * image[...]
        image[...] = image_next[...] - rate0 * resid[...]
    with scope("sums1"):
        q_now = image_next[...]
        sums_start(
            1,
            0,
            pack(
                fold(direct[...] * q_now),
                fold(resid[...] * q_now),
                fold(q_now * q_now),
                fold(resid[...] * resid_image[...]),
                fold(q_now * resid_image[...]),
            ),
        )
    with scope("start2b"):
        put_field(2, image[...], 0)
        start_field(2, 0)
        put_field(2, image[...], 1)
        start_field(2, 1)
        send_behind(2)
    with scope("diag2"):
        diag_products(2)
        w_now = image[...]
        local = fold(w_now * (own_part[...] + noise[...] * w_now))
    with scope("finish2"):
        finish_field(2)
    with scope("sums1b"):
        sums_start(1, 1, sums_finish(1, 0))
    with scope("cols2"):
        col_products(2, 0)
        send_ahead(2)
        total = col_products(2, middle)
        finish_ahead(2)
    with scope("sums2"):
        sums_start(2, 0, pack(local + 2.0 * quadratic(2, total)))
    with scope("rows2"):
        row_products(2, middle, lambda p: True, 0)
    with scope("rows2b"):
        row_products(2, 0, lambda p: True, 1)
    with scope("send2"):
        send_products(2)
    with scope("sums2b"):
        sums_start(2, 1, sums_finish(2, 0))
    with scope("sums1c"):
        sums_start(1, 2, sums_finish(1, 1))
    with scope("own2"):
        own_products(2)
    with scope("sums2d"):
        total = sums_finish(1, 2)
        curve1 = unpack(total, 0)
        cross1 = unpack(total, 1)
        square1 = unpack(total, 2)
        inner_rr = unpack(total, 3)
        inner_qr = unpack(total, 4)
        step1 = norm1 / curve1
        norm2 = norm1 - 2.0 * step1 * cross1 + step1 * step1 * square1
        mix1 = norm2 / norm1
        keep = 1.0 - step1 * rate0
        inner_ww = unpack(sums_finish(2, 1), 0)
        inner_wr = inner_qr - rate0 * inner_rr
        inner_wq = square1 - rate0 * cross1
        curve2 = (
            step1 * step1 * inner_ww
            + keep * keep * inner_rr
            + mix1 * mix1 * curve1
            - 2.0 * keep * step1 * inner_wr
            + 2.0 * keep * mix1 * cross1
            - 2.0 * step1 * mix1 * inner_wq
        )
        step2 = norm2 / curve2
        r_now = resid[...] - step1 * image_next[...]
        d_now = r_now + mix1 * direct[...]
        sol_ref[...] = step0 * base[...] + step1 * direct[...] + step2 * d_now
        resid[...] = r_now - step2 * (keep * resid_image[...] + mix1 * image_next[...])
    with scope("take2"):
        take_products(2, image, twice)
        res_ref[...] = resid[...] + (step2 * step1) * twice[...]

    with scope("drain"):
        for k in range(ITERS):
            drain_field(k)
            drain_products(k)
            sums_drain(k)


def solution(mesh):
    tiles, subs = mesh.shape["tile"], mesh.shape["sub"]
    side = math.isqrt(tiles // 2)

    def on_device(right_side, point_order, noise_var, block_pairs, pair_blocks, diag_blocks):
        rhs, points = right_side.shape
        slots, block = pair_blocks.shape[:2]
        blk_dev = diag_blocks.shape[0]
        cfg = (tiles, subs, side, blk_dev, block, slots, rhs)
        members = 2 * subs + max(2 * side, tiles // 2)
        vec = pltpu.VMEM((rhs, points), F32)
        row = pltpu.VMEM((ITERS, blk_dev, rhs, block), BF16)
        dma = pltpu.SemaphoreType.DMA
        return pl.pallas_call(
            functools.partial(kernel, cfg),
            out_shape=(jax.ShapeDtypeStruct((rhs, points), F32),) * 2,
            in_specs=[pl.BlockSpec(memory_space=pltpu.MemorySpace.HBM)] * 6,
            out_specs=(pl.BlockSpec(memory_space=pltpu.VMEM),) * 2,
            scratch_shapes=[
                vec,
                pltpu.VMEM((1, points), jnp.int32),
                pltpu.VMEM((1, points), F32),
                pltpu.SMEM((2, slots), jnp.int32),
                pltpu.VMEM((slots, block, block), BF16),
                pltpu.VMEM((blk_dev, block, block), BF16),
                vec,
                vec,
                vec,
                vec,
                vec,
                vec,
                vec,
                vec,
                pltpu.VMEM((ITERS, 2, (subs + 1) * blk_dev, rhs, LANES), BF16),
                pltpu.VMEM((ITERS, 2, blk_dev, rhs, LANES), BF16),
                pltpu.VMEM((1 + slots, rhs, block), F32),
                pltpu.VMEM((1 + slots, rhs, block), F32),
                pltpu.VMEM((subs * blk_dev, rhs, block), F32),
                pltpu.VMEM((slots, block, block), BF16),
                pltpu.VMEM((ITERS, 3, blk_dev, rhs, block), BF16),
                pltpu.VMEM((ITERS, 3, blk_dev, rhs, block), BF16),
                row,
                row,
                pltpu.VMEM((16, LANES), jnp.int32),
                pltpu.SMEM((16, LANES), jnp.int32),
                pltpu.VMEM((ITERS, members, 1, LANES), F32),
                dma((5,)),
                dma,
                dma,
                dma((ITERS,)),
                dma((ITERS, 2, 3)),
                dma((ITERS,)),
                dma((ITERS,)),
                dma((ITERS,)),
                dma((ITERS,)),
                dma((ITERS,)),
                dma((ITERS,)),
                dma((ITERS, 3)),
                dma((ITERS, 3)),
            ],
            compiler_params=pltpu.CompilerParams(
                collective_id=0, has_side_effects=True, vmem_limit_bytes=50 << 20
            ),
            name="block_pair_solve",
        )(
            *(
                pltpu.with_memory_space_constraint(value, pltpu.MemorySpace.HBM)
                for value in (
                    right_side,
                    point_order,
                    noise_var.reshape(1, -1),
                    block_pairs.T,
                    pair_blocks,
                    diag_blocks,
                )
            )
        )

    both = ("tile", "sub")
    return jax.shard_map(
        on_device,
        mesh=mesh,
        in_specs=(
            P(None, both),
            P(both, None),
            P(both),
            P(both, None),
            P(both, None, None),
            P(both, None, None),
        ),
        out_specs=(P(None, both), P(None, both)),
        check_vma=False,
    )
```

```python
import functools
import math

import jax
import jax.numpy as jnp
from jax import lax
from jax.experimental import pallas as pl
from jax.experimental.pallas import tpu as pltpu
from jax.sharding import PartitionSpec as P

ITERS = 3
PARTS = 6
LANES = 128
F32 = jnp.float32
BF16 = jnp.bfloat16
MESH = pl.DeviceIdType.MESH


def scope(name):
    return jax.named_scope(name)


def kernel(
    cfg,
    right_hbm,
    order_hbm,
    noise_hbm,
    pairs_hbm,
    blocks_hbm,
    diag_hbm,
    sol_ref,
    res_ref,
    right,
    order,
    noise,
    pairs,
    blocks,
    diag,
    base,
    image,
    twice,
    resid,
    direct,
    image_next,
    resid_image,
    own_part,
    field_low,
    field_high,
    field_ahead,
    col_out,
    row_out,
    half_sums,
    turned,
    parts_out,
    parts_in,
    to_ahead,
    from_behind,
    table_vec,
    table,
    sums,
    in_sem,
    blocks_sem,
    table_sem,
    field_send,
    field_recv,
    ahead_send,
    ahead_recv,
    part_send,
    part_recv,
    behind_send,
    behind_recv,
    sums_send,
    sums_recv,
):
    tiles, subs, side, blk_dev, block, slots, rhs = cfg
    t = lax.axis_index("tile")
    s = lax.axis_index("sub")
    core = lax.rem(t, 2)
    above = lax.rem(s + 1, subs)
    below = lax.rem(s + subs - 1, subs)
    across = lax.rem(s + 2, subs)
    has_behind = t > 0
    has_ahead = t < tiles - 1

    fields = (field_low, field_high)
    loads = [
        pltpu.make_async_copy(right_hbm, right, in_sem.at[0]),
        pltpu.make_async_copy(order_hbm, order, in_sem.at[1]),
        pltpu.make_async_copy(pairs_hbm, pairs, in_sem.at[2]),
        pltpu.make_async_copy(noise_hbm, noise, in_sem.at[3]),
        pltpu.make_async_copy(diag_hbm, diag, in_sem.at[4]),
    ]
    step = slots // PARTS
    block_loads = [
        pltpu.make_async_copy(
            blocks_hbm.at[pl.ds(i * step, step)],
            blocks.at[pl.ds(i * step, step)],
            blocks_sem,
        )
        for i in range(PARTS)
    ]
    for copy in loads[:2]:
        copy.start()

    group = core * subs + s
    chip_x = lax.rem(t // 2, side)
    chip_y = t // (2 * side)

    def column_partner(index):
        return (t - core + index // subs, lax.rem(index, subs))

    def x_partner(index):
        return ((chip_y * side + index) * 2 + core, s)

    def y_partner(index):
        return ((index * side + chip_x) * 2 + core, s)

    def plane_partner(index):
        return (index * 2 + core, s)

    stages = (
        (2 * subs, group, column_partner, 0),
        (side, chip_x, x_partner, 2 * subs),
        (side, chip_y, y_partner, 2 * subs + side),
    )
    last_stages = (stages[0], (tiles // 2, t // 2, plane_partner, 2 * subs))

    def stages_of(k):
        return last_stages if k == ITERS - 1 else stages

    barrier = pltpu.get_barrier_semaphore()
    greeted = 0
    for count, mine, partner, unused in stages:
        for j in range(1, count):
            pl.semaphore_signal(
                barrier, inc=1, device_id=partner(lax.rem(mine + j, count)), device_id_type=MESH
            )
            greeted += 1
    far_ahead = (core == 1) & has_ahead
    far_behind = (core == 0) & has_behind

    @pl.when(far_ahead)
    def _():
        pl.semaphore_signal(barrier, inc=1, device_id=(t + 1, s), device_id_type=MESH)

        @pl.when(s > 0)
        def _():
            pl.semaphore_signal(barrier, inc=1, device_id=(t + 1, 0), device_id_type=MESH)

    @pl.when(far_behind)
    def _():
        pl.semaphore_signal(barrier, inc=1, device_id=(t - 1, s), device_id_type=MESH)

        @pl.when(s == 0)
        def _():
            for j in range(1, subs):
                pl.semaphore_signal(barrier, inc=1, device_id=(t - 1, j), device_id_type=MESH)

    for copy in block_loads[:1]:
        copy.start()
    for copy in loads[2:]:
        copy.start()
    for copy in block_loads[1:]:
        copy.start()

    chunks = right.shape[1] // LANES

    def permute(i, carry):
        for u in range(4):
            chunk = (i % (chunks // 8) * 4 + u) * 2 + i // (chunks // 8)
            at = pl.multiple_of(chunk * LANES, LANES)
            index = jnp.broadcast_to(order[:, pl.ds(at, LANES)], (rhs, LANES))
            low = lax.bitwise_and(index, LANES - 1)
            high = lax.shift_right_logical(index, 7)
            out = jnp.zeros((rhs, LANES), F32)
            for h in range(chunks):
                picked = jnp.take_along_axis(right[:, h * LANES : (h + 1) * LANES], low, axis=1)
                out = jnp.where(high == h, picked, out)
            base[:, pl.ds(at, LANES)] = out
        return carry

    def put_field(k, values, h):
        for b in range(blk_dev):
            at = b * block + h * LANES
            fields[h][k, s * blk_dev + b] = values[:, at : at + LANES].astype(BF16)

    def whole(k, q):
        return jnp.concatenate([field_low[k, q], field_high[k, q]], axis=1)

    def remote(src, dst, send, recv, target):
        return pltpu.make_async_remote_copy(
            src_ref=src,
            dst_ref=dst,
            send_sem=send,
            recv_sem=recv,
            device_id=target,
            device_id_type=MESH,
        )

    targets = (across, above, below)
    sources = (across, below, above)

    def field_copy(k, row, h, n):
        part = fields[h].at[k, pl.ds(row * blk_dev, blk_dev)]
        return remote(part, part, field_send.at[k], field_recv.at[k, h, n], (t, targets[n]))

    def ahead_copy(k, h, to):
        return remote(
            fields[h].at[k, pl.ds(0, blk_dev)],
            field_ahead.at[k, h],
            ahead_send.at[k],
            ahead_recv.at[k],
            (t - 1, to),
        )

    def ahead_waits(k):
        both = field_ahead.at[k]
        return remote(both, both, ahead_send.at[k], ahead_recv.at[k], (t, above))

    def pass_back(k, row, h):
        @pl.when((row == 0) & (core == 1))
        def _():
            ahead_copy(k, h, s).start()

    def send_behind(k):
        @pl.when((s == 0) & far_behind)
        def _():
            for h in range(2):
                for j in (2, 1, 3, 0):
                    ahead_copy(k, h, j).start()

    def start_field(k, h):
        for n in range(3):
            field_copy(k, s, h, n).start()
        pass_back(k, s, h)

    def finish_field(k, h):
        for n in (1, 2, 0):
            field_copy(k, sources[n], h, n).wait_recv()
            pass_back(k, sources[n], h)

    def finish_ahead(k):
        @pl.when(has_ahead)
        def _():
            ahead_waits(k).wait_recv()

        for h in range(2):
            for b in range(blk_dev):
                fields[h][k, subs * blk_dev + b] = field_ahead[k, h, b]

    def drain_field(k):
        sent = parts_out.at[k]
        remote(sent, sent, field_send.at[k], field_recv.at[k, 0, 0], (t, above)).wait_send()

        @pl.when(core == 1)
        def _():
            ahead_waits(k).wait_send()

        @pl.when((s == 0) & far_behind)
        def _():
            sent = field_low.at[pl.ds(0, 2), pl.ds(0, subs * blk_dev)]
            remote(sent, sent, ahead_send.at[k], ahead_recv.at[k], (t, above)).wait_send()

    def sums_start(k, stage, values):
        count, mine, partner, offset = stages_of(k)[stage]
        sums[k, offset + mine] = values
        own = sums.at[k, offset + mine]
        for j in range(1, count):
            remote(
                own,
                own,
                sums_send.at[k, stage],
                sums_recv.at[k, stage],
                partner(lax.rem(mine + j, count)),
            ).start()

    def sums_waits(k, stage):
        count, mine, partner, offset = stages_of(k)[stage]
        others = sums.at[k, pl.ds(offset, count - 1)]
        return remote(
            others, others, sums_send.at[k, stage], sums_recv.at[k, stage], (t, above)
        )

    def sums_finish(k, stage):
        count, mine, partner, offset = stages_of(k)[stage]
        sums_waits(k, stage).wait_recv()
        total = sums[k, offset]
        for j in range(1, count):
            total = total + sums[k, offset + j]
        return total

    def sums_drain(k):
        for stage in range(len(stages_of(k))):
            sums_waits(k, stage).wait_send()

    def fold(values):
        parts = [values[:, i : i + LANES] for i in range(0, values.shape[1], LANES)]
        while len(parts) > 1:
            parts = [a + b for a, b in zip(parts[::2], parts[1::2])]
        return parts[0]

    spot = lax.broadcasted_iota(jnp.int32, (rhs, LANES), 1) - lax.broadcasted_iota(
        jnp.int32, (rhs, LANES), 0
    )

    def pack(*folded):
        out = jnp.zeros((rhs, LANES), F32)
        for n, values in enumerate(folded):
            column = jnp.sum(values, axis=1, keepdims=True)
            out = jnp.where(spot == n * rhs, column, out)
        return jnp.sum(out, axis=0, keepdims=True)

    def unpack(total, n):
        wide = jnp.broadcast_to(total, (rhs, LANES))
        return jnp.sum(jnp.where(spot == n * rhs, wide, 0.0), axis=1, keepdims=True)

    first = t * (subs * blk_dev)
    middle = slots // 2
    tile_blocks = subs * blk_dev

    def build_table():
        shape = (8, LANES)
        sub_id = lax.broadcasted_iota(jnp.int32, shape, 0)
        lane_id = lax.broadcasted_iota(jnp.int32, shape, 1)
        ids = sub_id * LANES + lane_id

        def add_slot(i, carry):
            found, listed, low, high = carry
            for u in range(8):
                p = i * 8 + u
                row = pairs[0, p]
                col = pairs[1, p]
                live = row >= 0
                reach = jnp.where(col - first >= tile_blocks, 1, 0)
                place = jnp.where(reach == 1, low, high)
                low = low + reach
                high = high - (1 - reach)
                apart = col - row
                kind = jnp.where(apart == 1, 0, apart - (blk_dev - 2))
                key_col = jnp.where(live, (col - first) * 4 + kind, -1)
                key_row = jnp.where(live, (row - first) * 4 + kind + 4 * LANES, -1)
                found = jnp.where((ids == key_col) | (ids == key_row), place + 1, found)
                entry = jnp.where(
                    sub_id == 0,
                    p,
                    jnp.where(
                        sub_id == 1, jnp.maximum(row - first, 0), jnp.maximum(col - first, 0)
                    ),
                )
                listed = jnp.where(lane_id == place, entry, listed)
            return found, listed, low, high

        zeros = jnp.zeros(shape, jnp.int32)
        found, listed, unused_low, unused_high = lax.fori_loop(
            0, slots // 8, add_slot, (zeros, zeros, jnp.int32(0), jnp.int32(slots - 1))
        )
        table_vec[0:8] = found
        table_vec[8:16] = listed
        move = pltpu.make_async_copy(table_vec, table, table_sem)
        move.start()
        move.wait()
        col_out[0] = jnp.zeros((rhs, block), F32)
        row_out[0] = jnp.zeros((rhs, block), F32)

    def diag_products(k):
        def body(i, carry):
            for u in range(8):
                b = i * 8 + u
                at = pl.multiple_of(b * block, block)
                own_part[:, pl.ds(at, block)] = jnp.dot(
                    whole(k, s * blk_dev + b), diag[b], preferred_element_type=F32
                )
            return carry

        lax.fori_loop(0, blk_dev // 8, body, 0)

    def listed_sum(out, line, q, kinds):
        at = q * 4
        row = line + at // LANES
        lane = lax.rem(at, LANES)
        parts = [out[table[row, lane + n]] for n in kinds]
        while len(parts) > 1:
            paired = [x + y for x, y in zip(parts[::2], parts[1::2])]
            parts = paired + parts[len(paired) * 2 :]
        return parts[0]

    across_rows = (((1,), (0,)), ((), ()))
    across_cols = (((1,), (1,)), ((), ()))

    def turn(p):
        turned[p] = blocks[table[8, p]].T

    def dot(left, right_block, dims):
        return lax.dot_general(left, right_block, dims, preferred_element_type=F32)

    def early_cols(k, low, also=()):
        for u in range(middle):
            p = low + u
            left = field_low[k, table[9, p]]
            col_out[1 + p] = dot(left, blocks[table[8, p], :LANES], across_rows)
            if u % 2 == 0 and u // 2 < len(also):
                turn(also[u // 2])

    def col_products(k, low):
        total = jnp.zeros((rhs, block), F32)
        for u in range(middle):
            p = low + u
            left = field_high[k, table[9, p]]
            out = col_out[1 + p] + dot(left, blocks[table[8, p], LANES:], across_rows)
            col_out[1 + p] = out
            if k == ITERS - 1 and low > 0:
                total = total + out * whole(k, table[10, p]).astype(F32)
        return total

    def early_rows(k):
        for p in range(middle, slots):
            left = field_low[k, table[10, p]]
            row_out[1 + p] = dot(left, turned[p, :LANES], across_rows)

    def row_products(k, low, is_turned, line, is_early, also=()):
        share = tile_blocks // 2
        for u in range(middle):
            p = low + u
            if is_early:
                left = field_high[k, table[10, p]]
                out = row_out[1 + p] + dot(left, turned[p, LANES:], across_rows)
            elif is_turned(p):
                out = dot(whole(k, table[10, p]), turned[p], across_rows)
            else:
                out = dot(whole(k, table[10, p]), blocks[table[8, p]], across_cols)
            row_out[1 + p] = out
            if u < share:
                q = line * share + u
                half_sums[q] = listed_sum(col_out, 0, q, range(4))
            if u % 2 == 0 and u // 2 < len(also):
                turn(also[u // 2])

    def quadratic(k, total):
        def body(i, total):
            for u in range(8):
                p = i * 8 + u
                total = total + col_out[1 + p] * whole(k, table[10, p]).astype(F32)
            return total

        return fold(lax.fori_loop(0, middle // 8, body, total))

    def partial_sum(row, b):
        q = row * blk_dev + b
        return half_sums[q] + listed_sum(row_out, 4, q, range(4))

    def part_copy(k, n):
        return remote(
            parts_out.at[k, n], parts_in.at[k, n], part_send.at[k], part_recv.at[k], (t, targets[n])
        )

    def part_waits(k):
        return remote(
            parts_out.at[k], parts_in.at[k], part_send.at[k], part_recv.at[k], (t, above)
        )

    def behind_copy(k):
        return remote(
            to_ahead.at[k],
            from_behind.at[k],
            behind_send.at[k],
            behind_recv.at[k],
            (t + 1, s),
        )

    def send_ahead(k):
        @pl.when(has_ahead)
        def _():
            def body(i, carry):
                for u in range(8):
                    b = i * 8 + u
                    q = subs * blk_dev + b
                    to_ahead[k, b] = listed_sum(col_out, 0, q, (1, 2, 3)).astype(BF16)
                return carry

            lax.fori_loop(0, blk_dev // 8, body, 0)
            behind_copy(k).start()

    def send_products(k):
        @pl.when(has_behind)
        def _():
            behind_copy(k).wait_recv()

        for b in range(blk_dev):
            half_sums[b] = half_sums[b] + from_behind[k, b].astype(F32)

        for n in range(3):

            def body(i, carry):
                for u in range(8):
                    b = i * 8 + u
                    parts_out[k, n, b] = partial_sum(targets[n], b).astype(BF16)
                return carry

            lax.fori_loop(0, blk_dev // 8, body, 0)
            part_copy(k, n).start()

    def own_products(k):
        def body(i, carry):
            for u in range(4):
                b = i * 4 + u
                at = pl.ds(pl.multiple_of(b * block, block), block)
                own_part[:, at] = own_part[:, at] + partial_sum(s, b)
            return carry

        lax.fori_loop(0, blk_dev // 4, body, 0)

    def take_products(k, vector, out):
        part_waits(k).wait_recv()
        for b in range(blk_dev):
            at = slice(b * block, (b + 1) * block)
            total = parts_in[k, 0, b].astype(F32) + parts_in[k, 1, b].astype(F32)
            total = total + parts_in[k, 2, b].astype(F32)
            out[:, at] = total + (own_part[:, at] + noise[:, at] * vector[:, at])

    def drain_products(k):
        part_waits(k).wait_send()

        @pl.when(has_ahead)
        def _():
            behind_copy(k).wait_send()


    loads[0].wait()
    loads[1].wait()
    with scope("permute0"):
        lax.fori_loop(0, chunks // 8, permute, 0)
        put_field(0, base[...], 0)
    with scope("barrier"):
        pl.semaphore_wait(barrier, greeted
            + jnp.where(far_ahead | far_behind, 1, 0)
            + jnp.where(far_ahead & (s > 0), 1, 0)
            + jnp.where(far_behind & (s == 0), subs - 1, 0))
    start_field(0, 0)
    with scope("permute1"):
        lax.fori_loop(chunks // 8, chunks // 4, permute, 0)
        put_field(0, base[...], 1)
    start_field(0, 1)
    send_behind(0)

    @pl.when(jnp.logical_not(has_ahead))
    def _():
        for k in range(ITERS):
            field_ahead[k] = jnp.zeros((2, blk_dev, rhs, LANES), BF16)

    @pl.when(jnp.logical_not(has_behind))
    def _():
        for k in range(ITERS):
            from_behind[k] = jnp.zeros((blk_dev, rhs, block), BF16)

    loads[2].wait()
    with scope("table"):
        build_table()
    loads[4].wait()
    with scope("diag0"):
        diag_products(0)
    pltpu.make_async_copy(blocks_hbm, blocks, blocks_sem).wait()
    with scope("finish0"):
        finish_field(0, 0)
    with scope("early0"):
        quarter = middle // 2
        early_cols(0, 0, range(middle, middle + quarter))
        early_cols(0, middle, range(middle + quarter, slots))
        early_rows(0)
    with scope("finish0b"):
        finish_field(0, 1)
    with scope("cols0"):
        col_products(0, 0)
        send_ahead(0)
        col_products(0, middle)
    with scope("rows0"):
        row_products(0, middle, lambda p: True, 0, True, range(quarter))
        finish_ahead(0)
        row_products(0, 0, lambda p: p < quarter, 1, False, range(quarter, middle))
    with scope("send0"):
        send_products(0)
    with scope("own0"):
        own_products(0)
    loads[3].wait()
    with scope("take0"):
        take_products(0, base, image)

    with scope("sums0"):
        b_now = base[...]
        q_now = image[...]
        sums_start(0, 0, pack(fold(b_now * b_now), fold(b_now * q_now), fold(q_now * q_now)))
    with scope("start1"):
        put_field(1, image[...], 0)
        start_field(1, 0)
        put_field(1, image[...], 1)
        start_field(1, 1)
        send_behind(1)
    with scope("diag1"):
        diag_products(1)
    with scope("finish1"):
        finish_field(1, 0)
    with scope("early1"):
        early_cols(1, 0)
        early_cols(1, middle)
        early_rows(1)
    with scope("finish1b"):
        finish_field(1, 1)
    with scope("sums0b"):
        sums_start(0, 1, sums_finish(0, 0))
    with scope("cols1"):
        col_products(1, 0)
        send_ahead(1)
        col_products(1, middle)
    with scope("rows1"):
        row_products(1, middle, lambda p: True, 0, True)
    with scope("rows1b"):
        finish_ahead(1)
        row_products(1, 0, lambda p: True, 1, False)
    with scope("send1"):
        send_products(1)
    with scope("sums0c"):
        sums_start(0, 2, sums_finish(0, 1))
    with scope("own1"):
        own_products(1)
    with scope("sums0d"):
        total = sums_finish(0, 2)
        norm0 = unpack(total, 0)
        curve0 = unpack(total, 1)
        square0 = unpack(total, 2)
        step0 = norm0 / curve0
        rate0 = curve0 / norm0
        norm1 = norm0 - 2.0 * step0 * curve0 + step0 * step0 * square0
        mix0 = norm1 / norm0
        resid[...] = base[...] - step0 * image[...]
        direct[...] = resid[...] + mix0 * base[...]
    with scope("take1"):
        take_products(1, image, twice)

    with scope("start2"):
        resid_image[...] = image[...] - step0 * twice[...]
        image_next[...] = resid_image[...] + mix0 * image[...]
        image[...] = image_next[...] - rate0 * resid[...]
    with scope("sums1"):
        q_now = image_next[...]
        sums_start(
            1,
            0,
            pack(
                fold(direct[...] * q_now),
                fold(resid[...] * q_now),
                fold(q_now * q_now),
                fold(resid[...] * resid_image[...]),
                fold(q_now * resid_image[...]),
            ),
        )
    with scope("start2b"):
        put_field(2, image[...], 0)
        start_field(2, 0)
        put_field(2, image[...], 1)
        start_field(2, 1)
        send_behind(2)
    with scope("diag2"):
        diag_products(2)
        w_now = image[...]
        local = fold(w_now * (own_part[...] + noise[...] * w_now))
    with scope("finish2"):
        finish_field(2, 0)
    with scope("early2"):
        early_cols(2, 0)
        early_cols(2, middle)
    with scope("finish2b"):
        finish_field(2, 1)
    with scope("sums1b"):
        sums_start(1, 1, sums_finish(1, 0))
    with scope("cols2"):
        col_products(2, 0)
        send_ahead(2)
        total = col_products(2, middle)
        finish_ahead(2)
    with scope("sums2"):
        sums_start(2, 0, pack(local + 2.0 * quadratic(2, total)))
    with scope("rows2"):
        row_products(2, middle, lambda p: True, 0, False)
    with scope("rows2b"):
        row_products(2, 0, lambda p: True, 1, False)
    with scope("send2"):
        send_products(2)
    with scope("sums2b"):
        sums_start(2, 1, sums_finish(2, 0))
    with scope("sums1c"):
        sums_start(1, 2, sums_finish(1, 1))
    with scope("own2"):
        own_products(2)
    with scope("sums2d"):
        total = sums_finish(1, 2)
        curve1 = unpack(total, 0)
        cross1 = unpack(total, 1)
        square1 = unpack(total, 2)
        inner_rr = unpack(total, 3)
        inner_qr = unpack(total, 4)
        step1 = norm1 / curve1
        norm2 = norm1 - 2.0 * step1 * cross1 + step1 * step1 * square1
        mix1 = norm2 / norm1
        keep = 1.0 - step1 * rate0
        inner_ww = unpack(sums_finish(2, 1), 0)
        inner_wr = inner_qr - rate0 * inner_rr
        inner_wq = square1 - rate0 * cross1
        curve2 = (
            step1 * step1 * inner_ww
            + keep * keep * inner_rr
            + mix1 * mix1 * curve1
            - 2.0 * keep * step1 * inner_wr
            + 2.0 * keep * mix1 * cross1
            - 2.0 * step1 * mix1 * inner_wq
        )
        step2 = norm2 / curve2
        r_now = resid[...] - step1 * image_next[...]
        d_now = r_now + mix1 * direct[...]
        sol_ref[...] = step0 * base[...] + step1 * direct[...] + step2 * d_now
        resid[...] = r_now - step2 * (keep * resid_image[...] + mix1 * image_next[...])
    with scope("take2"):
        take_products(2, image, twice)
        res_ref[...] = resid[...] + (step2 * step1) * twice[...]

    with scope("drain"):
        for k in range(ITERS):
            drain_field(k)
            drain_products(k)
            sums_drain(k)


def solution(mesh):
    tiles, subs = mesh.shape["tile"], mesh.shape["sub"]
    side = math.isqrt(tiles // 2)

    def on_device(right_side, point_order, noise_var, block_pairs, pair_blocks, diag_blocks):
        rhs, points = right_side.shape
        slots, block = pair_blocks.shape[:2]
        blk_dev = diag_blocks.shape[0]
        cfg = (tiles, subs, side, blk_dev, block, slots, rhs)
        members = 2 * subs + max(2 * side, tiles // 2)
        vec = pltpu.VMEM((rhs, points), F32)
        row = pltpu.VMEM((ITERS, blk_dev, rhs, block), BF16)
        dma = pltpu.SemaphoreType.DMA
        return pl.pallas_call(
            functools.partial(kernel, cfg),
            out_shape=(jax.ShapeDtypeStruct((rhs, points), F32),) * 2,
            in_specs=[pl.BlockSpec(memory_space=pltpu.MemorySpace.HBM)] * 6,
            out_specs=(pl.BlockSpec(memory_space=pltpu.VMEM),) * 2,
            scratch_shapes=[
                vec,
                pltpu.VMEM((1, points), jnp.int32),
                pltpu.VMEM((1, points), F32),
                pltpu.SMEM((2, slots), jnp.int32),
                pltpu.VMEM((slots, block, block), BF16),
                pltpu.VMEM((blk_dev, block, block), BF16),
                vec,
                vec,
                vec,
                vec,
                vec,
                vec,
                vec,
                vec,
                pltpu.VMEM((ITERS, (subs + 1) * blk_dev, rhs, LANES), BF16),
                pltpu.VMEM((ITERS, (subs + 1) * blk_dev, rhs, LANES), BF16),
                pltpu.VMEM((ITERS, 2, blk_dev, rhs, LANES), BF16),
                pltpu.VMEM((1 + slots, rhs, block), F32),
                pltpu.VMEM((1 + slots, rhs, block), F32),
                pltpu.VMEM((subs * blk_dev, rhs, block), F32),
                pltpu.VMEM((slots, block, block), BF16),
                pltpu.VMEM((ITERS, 3, blk_dev, rhs, block), BF16),
                pltpu.VMEM((ITERS, 3, blk_dev, rhs, block), BF16),
                row,
                row,
                pltpu.VMEM((16, LANES), jnp.int32),
                pltpu.SMEM((16, LANES), jnp.int32),
                pltpu.VMEM((ITERS, members, 1, LANES), F32),
                dma((5,)),
                dma,
                dma,
                dma((ITERS,)),
                dma((ITERS, 2, 3)),
                dma((ITERS,)),
                dma((ITERS,)),
                dma((ITERS,)),
                dma((ITERS,)),
                dma((ITERS,)),
                dma((ITERS,)),
                dma((ITERS, 3)),
                dma((ITERS, 3)),
            ],
            compiler_params=pltpu.CompilerParams(
                collective_id=0, has_side_effects=True, vmem_limit_bytes=50 << 20
            ),
            name="block_pair_solve",
        )(
            *(
                pltpu.with_memory_space_constraint(value, pltpu.MemorySpace.HBM)
                for value in (
                    right_side,
                    point_order,
                    noise_var.reshape(1, -1),
                    block_pairs.T,
                    pair_blocks,
                    diag_blocks,
                )
            )
        )

    both = ("tile", "sub")
    return jax.shard_map(
        on_device,
        mesh=mesh,
        in_specs=(
            P(None, both),
            P(both, None),
            P(both),
            P(both, None),
            P(both, None, None),
            P(both, None, None),
        ),
        out_specs=(P(None, both), P(None, both)),
        check_vma=False,
    )
```

```python
import functools
import math

import jax
import jax.numpy as jnp
from jax import lax
from jax.experimental import pallas as pl
from jax.experimental.pallas import tpu as pltpu
from jax.sharding import PartitionSpec as P

ITERS = 3
PARTS = 6
LANES = 128
F32 = jnp.float32
BF16 = jnp.bfloat16
MESH = pl.DeviceIdType.MESH


def scope(name):
    return jax.named_scope(name)


def kernel(
    cfg,
    right_hbm,
    order_hbm,
    noise_hbm,
    pairs_hbm,
    blocks_hbm,
    diag_hbm,
    sol_ref,
    res_ref,
    right,
    order,
    noise,
    pairs,
    blocks,
    diag,
    base,
    image,
    twice,
    resid,
    direct,
    image_next,
    resid_image,
    own_part,
    field_low,
    field_high,
    field_ahead,
    col_out,
    row_out,
    half_sums,
    turned,
    parts_out,
    parts_in,
    to_ahead,
    from_behind,
    table_vec,
    table,
    sums,
    in_sem,
    blocks_sem,
    table_sem,
    field_send,
    field_recv,
    ahead_send,
    ahead_recv,
    part_send,
    part_recv,
    behind_send,
    behind_recv,
    sums_send,
    sums_recv,
):
    tiles, subs, side, blk_dev, block, slots, rhs = cfg
    t = lax.axis_index("tile")
    s = lax.axis_index("sub")
    core = lax.rem(t, 2)
    above = jnp.where(s == subs - 1, 0, s + 1)
    below = jnp.where(s == 0, subs - 1, s - 1)
    across = jnp.where(s >= subs - 2, s + 2 - subs, s + 2)
    has_behind = t > 0
    has_ahead = t < tiles - 1

    fields = (field_low, field_high)
    loads = [
        pltpu.make_async_copy(right_hbm, right, in_sem.at[0]),
        pltpu.make_async_copy(order_hbm, order, in_sem.at[1]),
        pltpu.make_async_copy(pairs_hbm, pairs, in_sem.at[2]),
        pltpu.make_async_copy(noise_hbm, noise, in_sem.at[3]),
        pltpu.make_async_copy(diag_hbm, diag, in_sem.at[4]),
    ]
    step = slots // PARTS
    block_loads = [
        pltpu.make_async_copy(
            blocks_hbm.at[pl.ds(i * step, step)],
            blocks.at[pl.ds(i * step, step)],
            blocks_sem,
        )
        for i in range(PARTS)
    ]
    for copy in loads[:3]:
        copy.start()

    def wrap(index, count):
        return jnp.where(index >= count, index - count, index)

    group = core * subs + s
    chip_x = lax.rem(t // 2, side)
    chip_y = t // (2 * side)
    far_ahead = (core == 1) & has_ahead
    far_behind = (core == 0) & has_behind
    other_core = t + 1 - 2 * core
    column = [(t, wrap(s + j, subs)) for j in range(1, subs)] + [
        (other_core, wrap(s + j, subs)) for j in range(subs)
    ]
    along_x = [((chip_y * side + wrap(chip_x + j, side)) * 2 + core, s) for j in range(1, side)]
    along_y = [((wrap(chip_y + j, side) * side + chip_x) * 2 + core, s) for j in range(1, side)]
    plane = []
    for i in range(side):
        for j in range(side):
            if i or j:
                at = wrap(chip_y + i, side) * side + wrap(chip_x + j, side)
                plane.append((at * 2 + core, s))

    stages = (
        (group, column, 0),
        (chip_x, along_x, 2 * subs),
        (chip_y, along_y, 2 * subs + side),
    )
    last_stages = (stages[0], (t // 2, plane, 2 * subs))

    def stages_of(k):
        return last_stages if k == ITERS - 1 else stages

    barrier = pltpu.get_barrier_semaphore()

    def greet(target):
        pl.semaphore_signal(barrier, inc=1, device_id=target, device_id_type=MESH)

    @pl.when(far_ahead)
    def _():
        @pl.when(s > 0)
        def _():
            greet((t + 1, 0))

        greet((t + 1, s))

    @pl.when(far_behind)
    def _():
        @pl.when(s == 0)
        def _():
            for j in range(1, subs):
                greet((t - 1, j))

        greet((t - 1, s))

    greeted = 0
    for unused, members, also_unused in stages:
        for target in members:
            greet(target)
            greeted += 1

    for copy in (loads[4], *block_loads, loads[3]):
        copy.start()

    chunks = right.shape[1] // LANES

    def permute(i, carry):
        for u in range(4):
            chunk = (i % (chunks // 8) * 4 + u) * 2 + i // (chunks // 8)
            at = pl.multiple_of(chunk * LANES, LANES)
            index = jnp.broadcast_to(order[:, pl.ds(at, LANES)], (rhs, LANES))
            low = lax.bitwise_and(index, LANES - 1)
            high = lax.shift_right_logical(index, 7)
            out = jnp.zeros((rhs, LANES), F32)
            for h in range(chunks):
                picked = jnp.take_along_axis(right[:, h * LANES : (h + 1) * LANES], low, axis=1)
                out = jnp.where(high == h, picked, out)
            base[:, pl.ds(at, LANES)] = out
        return carry

    def put_field(k, values, h):
        for b in range(blk_dev):
            at = b * block + h * LANES
            fields[h][k, s * blk_dev + b] = values[:, at : at + LANES].astype(BF16)

    def whole(k, q):
        return jnp.concatenate([field_low[k, q], field_high[k, q]], axis=1)

    def remote(src, dst, send, recv, target):
        return pltpu.make_async_remote_copy(
            src_ref=src,
            dst_ref=dst,
            send_sem=send,
            recv_sem=recv,
            device_id=target,
            device_id_type=MESH,
        )

    targets = (across, above, below)
    sources = (across, below, above)

    def field_copy(k, row, h, n):
        part = fields[h].at[k, pl.ds(row * blk_dev, blk_dev)]
        return remote(part, part, field_send.at[k], field_recv.at[k, h, n], (t, targets[n]))

    def ahead_copy(k, h, to):
        return remote(
            fields[h].at[k, pl.ds(0, blk_dev)],
            field_ahead.at[k, h],
            ahead_send.at[k],
            ahead_recv.at[k],
            (t - 1, to),
        )

    def ahead_waits(k):
        both = field_ahead.at[k]
        return remote(both, both, ahead_send.at[k], ahead_recv.at[k], (t, above))

    def pass_back(k, row, h):
        @pl.when((row == 0) & (core == 1))
        def _():
            ahead_copy(k, h, s).start()

    def send_behind(k):
        @pl.when((s == 0) & far_behind)
        def _():
            for h in range(2):
                for j in (2, 1, 3, 0):
                    ahead_copy(k, h, j).start()

    def start_field(k, h):
        for n in range(3):
            field_copy(k, s, h, n).start()
        pass_back(k, s, h)

    def finish_field(k, h):
        for n in (1, 2, 0):
            field_copy(k, sources[n], h, n).wait_recv()
            pass_back(k, sources[n], h)

    def finish_ahead(k):
        @pl.when(has_ahead)
        def _():
            ahead_waits(k).wait_recv()

        for h in range(2):
            for b in range(blk_dev):
                fields[h][k, subs * blk_dev + b] = field_ahead[k, h, b]

    def drain_field(k):
        sent = parts_out.at[k]
        remote(sent, sent, field_send.at[k], field_recv.at[k, 0, 0], (t, above)).wait_send()

        @pl.when(core == 1)
        def _():
            ahead_waits(k).wait_send()

        @pl.when((s == 0) & far_behind)
        def _():
            sent = field_low.at[pl.ds(0, 2), pl.ds(0, subs * blk_dev)]
            remote(sent, sent, ahead_send.at[k], ahead_recv.at[k], (t, above)).wait_send()

    def sums_start(k, stage, values):
        mine, members, offset = stages_of(k)[stage]
        sums[k, offset + mine] = values
        own = sums.at[k, offset + mine]
        for target in members:
            remote(own, own, sums_send.at[k, stage], sums_recv.at[k, stage], target).start()

    def sums_waits(k, stage):
        mine, members, offset = stages_of(k)[stage]
        others = sums.at[k, pl.ds(offset, len(members))]
        return remote(
            others, others, sums_send.at[k, stage], sums_recv.at[k, stage], (t, above)
        )

    def sums_finish(k, stage):
        mine, members, offset = stages_of(k)[stage]
        sums_waits(k, stage).wait_recv()
        total = sums[k, offset]
        for j in range(1, len(members) + 1):
            total = total + sums[k, offset + j]
        return total

    def sums_drain(k):
        for stage in range(len(stages_of(k))):
            sums_waits(k, stage).wait_send()

    def fold(values):
        parts = [values[:, i : i + LANES] for i in range(0, values.shape[1], LANES)]
        while len(parts) > 1:
            parts = [a + b for a, b in zip(parts[::2], parts[1::2])]
        return parts[0]

    spot = lax.broadcasted_iota(jnp.int32, (rhs, LANES), 1) - lax.broadcasted_iota(
        jnp.int32, (rhs, LANES), 0
    )

    def pack(*folded):
        out = jnp.zeros((rhs, LANES), F32)
        for n, values in enumerate(folded):
            column = jnp.sum(values, axis=1, keepdims=True)
            out = jnp.where(spot == n * rhs, column, out)
        return jnp.sum(out, axis=0, keepdims=True)

    def unpack(total, n):
        wide = jnp.broadcast_to(total, (rhs, LANES))
        return jnp.sum(jnp.where(spot == n * rhs, wide, 0.0), axis=1, keepdims=True)

    first = t * (subs * blk_dev)
    middle = slots // 2
    tile_blocks = subs * blk_dev

    def build_table():
        shape = (8, LANES)
        sub_id = lax.broadcasted_iota(jnp.int32, shape, 0)
        lane_id = lax.broadcasted_iota(jnp.int32, shape, 1)
        ids = sub_id * LANES + lane_id

        def add_slot(i, carry):
            found, listed, low, high = carry
            for u in range(8):
                p = i * 8 + u
                row = pairs[0, p]
                col = pairs[1, p]
                live = row >= 0
                reach = jnp.where(col - first >= tile_blocks, 1, 0)
                place = jnp.where(reach == 1, low, high)
                low = low + reach
                high = high - (1 - reach)
                apart = col - row
                kind = jnp.where(apart == 1, 0, apart - (blk_dev - 2))
                key_col = jnp.where(live, (col - first) * 4 + kind, -1)
                key_row = jnp.where(live, (row - first) * 4 + kind + 4 * LANES, -1)
                found = jnp.where((ids == key_col) | (ids == key_row), place + 1, found)
                entry = jnp.where(
                    sub_id == 0,
                    p,
                    jnp.where(
                        sub_id == 1, jnp.maximum(row - first, 0), jnp.maximum(col - first, 0)
                    ),
                )
                listed = jnp.where(lane_id == place, entry, listed)
            return found, listed, low, high

        zeros = jnp.zeros(shape, jnp.int32)
        found, listed, unused_low, unused_high = lax.fori_loop(
            0, slots // 8, add_slot, (zeros, zeros, jnp.int32(0), jnp.int32(slots - 1))
        )
        table_vec[0:8] = found
        table_vec[8:16] = listed
        move = pltpu.make_async_copy(table_vec, table, table_sem)
        move.start()
        move.wait()
        col_out[0] = jnp.zeros((rhs, block), F32)
        row_out[0] = jnp.zeros((rhs, block), F32)

    def diag_products(k):
        def body(i, carry):
            for u in range(8):
                b = i * 8 + u
                at = pl.multiple_of(b * block, block)
                own_part[:, pl.ds(at, block)] = jnp.dot(
                    whole(k, s * blk_dev + b), diag[b], preferred_element_type=F32
                )
            return carry

        lax.fori_loop(0, blk_dev // 8, body, 0)

    def listed_sum(out, line, q, kinds):
        at = q * 4
        if isinstance(q, int):
            row, lane = line + at // LANES, at % LANES
        else:
            row = line + lax.shift_right_logical(at, 7)
            lane = lax.bitwise_and(at, LANES - 1)
        parts = [out[table[row, lane + n]] for n in kinds]
        while len(parts) > 1:
            paired = [x + y for x, y in zip(parts[::2], parts[1::2])]
            parts = paired + parts[len(paired) * 2 :]
        return parts[0]

    across_rows = (((1,), (0,)), ((), ()))
    across_cols = (((1,), (1,)), ((), ()))

    def turn(p):
        turned[p] = blocks[table[8, p]].T

    def dot(left, right_block, dims):
        return lax.dot_general(left, right_block, dims, preferred_element_type=F32)

    def early_cols(k, low, also=()):
        for u in range(middle):
            p = low + u
            left = field_low[k, table[9, p]]
            col_out[1 + p] = dot(left, blocks[table[8, p], :LANES], across_rows)
            if u % 2 == 0 and u // 2 < len(also):
                turn(also[u // 2])

    def col_products(k, low):
        total = jnp.zeros((rhs, block), F32)
        for u in range(middle):
            p = low + u
            left = field_high[k, table[9, p]]
            out = col_out[1 + p] + dot(left, blocks[table[8, p], LANES:], across_rows)
            col_out[1 + p] = out
            if k == ITERS - 1 and low > 0:
                total = total + out * whole(k, table[10, p]).astype(F32)
        return total

    def early_rows(k):
        for p in range(middle, slots):
            left = field_low[k, table[10, p]]
            row_out[1 + p] = dot(left, turned[p, :LANES], across_rows)

    def row_products(k, low, is_turned, line, is_early, also=()):
        share = tile_blocks // 2
        for u in range(middle):
            p = low + u
            if is_early:
                left = field_high[k, table[10, p]]
                out = row_out[1 + p] + dot(left, turned[p, LANES:], across_rows)
            elif is_turned(p):
                out = dot(whole(k, table[10, p]), turned[p], across_rows)
            else:
                out = dot(whole(k, table[10, p]), blocks[table[8, p]], across_cols)
            row_out[1 + p] = out
            if u < share:
                q = line * share + u
                half_sums[q] = listed_sum(col_out, 0, q, range(4))
            if u % 2 == 0 and u // 2 < len(also):
                turn(also[u // 2])

    def quadratic(k, total):
        def body(i, total):
            for u in range(8):
                p = i * 8 + u
                total = total + col_out[1 + p] * whole(k, table[10, p]).astype(F32)
            return total

        return fold(lax.fori_loop(0, middle // 8, body, total))

    def partial_sum(row, b):
        q = row * blk_dev + b
        return half_sums[q] + listed_sum(row_out, 4, q, range(4))

    def part_copy(k, n):
        return remote(
            parts_out.at[k, n], parts_in.at[k, n], part_send.at[k], part_recv.at[k], (t, targets[n])
        )

    def part_waits(k):
        return remote(
            parts_out.at[k], parts_in.at[k], part_send.at[k], part_recv.at[k], (t, above)
        )

    def behind_copy(k):
        return remote(
            to_ahead.at[k],
            from_behind.at[k],
            behind_send.at[k],
            behind_recv.at[k],
            (t + 1, s),
        )

    def send_ahead(k):
        @pl.when(has_ahead)
        def _():
            def body(i, carry):
                for u in range(8):
                    b = i * 8 + u
                    q = subs * blk_dev + b
                    to_ahead[k, b] = listed_sum(col_out, 0, q, (1, 2, 3)).astype(BF16)
                return carry

            lax.fori_loop(0, blk_dev // 8, body, 0)
            behind_copy(k).start()

    def send_products(k):
        @pl.when(has_behind)
        def _():
            behind_copy(k).wait_recv()

        for b in range(blk_dev):
            half_sums[b] = half_sums[b] + from_behind[k, b].astype(F32)

        for n in range(3):

            def body(i, carry):
                for u in range(8):
                    b = i * 8 + u
                    parts_out[k, n, b] = partial_sum(targets[n], b).astype(BF16)
                return carry

            lax.fori_loop(0, blk_dev // 8, body, 0)
            part_copy(k, n).start()

    def own_products(k):
        def body(i, carry):
            for u in range(4):
                b = i * 4 + u
                at = pl.ds(pl.multiple_of(b * block, block), block)
                own_part[:, at] = own_part[:, at] + partial_sum(s, b)
            return carry

        lax.fori_loop(0, blk_dev // 4, body, 0)

    def take_products(k, vector, out):
        part_waits(k).wait_recv()
        for b in range(blk_dev):
            at = slice(b * block, (b + 1) * block)
            total = parts_in[k, 0, b].astype(F32) + parts_in[k, 1, b].astype(F32)
            total = total + parts_in[k, 2, b].astype(F32)
            out[:, at] = total + (own_part[:, at] + noise[:, at] * vector[:, at])

    def drain_products(k):
        part_waits(k).wait_send()

        @pl.when(has_ahead)
        def _():
            behind_copy(k).wait_send()


    loads[0].wait()
    loads[1].wait()
    with scope("permute0"):
        lax.fori_loop(0, chunks // 8, permute, 0)
        put_field(0, base[...], 0)
    with scope("barrier"):
        pl.semaphore_wait(barrier, greeted
            + jnp.where(far_ahead | far_behind, 1, 0)
            + jnp.where(far_ahead & (s > 0), 1, 0)
            + jnp.where(far_behind & (s == 0), subs - 1, 0))
    start_field(0, 0)
    with scope("permute1"):
        lax.fori_loop(chunks // 8, chunks // 4, permute, 0)
        put_field(0, base[...], 1)
    start_field(0, 1)
    send_behind(0)

    @pl.when(jnp.logical_not(has_ahead))
    def _():
        for k in range(ITERS):
            field_ahead[k] = jnp.zeros((2, blk_dev, rhs, LANES), BF16)

    @pl.when(jnp.logical_not(has_behind))
    def _():
        for k in range(ITERS):
            from_behind[k] = jnp.zeros((blk_dev, rhs, block), BF16)

    loads[2].wait()
    with scope("table"):
        build_table()
    loads[4].wait()
    with scope("diag0"):
        diag_products(0)
    pltpu.make_async_copy(blocks_hbm, blocks, blocks_sem).wait()
    with scope("finish0"):
        finish_field(0, 0)
    with scope("early0"):
        quarter = middle // 2
        early_cols(0, 0, range(middle, middle + quarter))
        early_cols(0, middle, range(middle + quarter, slots))
        early_rows(0)
    with scope("finish0b"):
        finish_field(0, 1)
    with scope("cols0"):
        col_products(0, 0)
        send_ahead(0)
        col_products(0, middle)
    with scope("rows0"):
        row_products(0, middle, lambda p: True, 0, True, range(quarter))
        finish_ahead(0)
        row_products(0, 0, lambda p: p < quarter, 1, False, range(quarter, middle))
    with scope("send0"):
        send_products(0)
    with scope("own0"):
        own_products(0)
    loads[3].wait()
    with scope("take0"):
        take_products(0, base, image)

    with scope("sums0"):
        b_now = base[...]
        q_now = image[...]
        sums_start(0, 0, pack(fold(b_now * b_now), fold(b_now * q_now), fold(q_now * q_now)))
    with scope("start1"):
        put_field(1, image[...], 0)
        start_field(1, 0)
        put_field(1, image[...], 1)
        start_field(1, 1)
        send_behind(1)
    with scope("diag1"):
        diag_products(1)
    with scope("finish1"):
        finish_field(1, 0)
    with scope("early1"):
        early_cols(1, 0)
        early_cols(1, middle)
        early_rows(1)
    with scope("finish1b"):
        finish_field(1, 1)
    with scope("sums0b"):
        sums_start(0, 1, sums_finish(0, 0))
    with scope("cols1"):
        col_products(1, 0)
        send_ahead(1)
        col_products(1, middle)
    with scope("rows1"):
        row_products(1, middle, lambda p: True, 0, True)
    with scope("rows1b"):
        finish_ahead(1)
        row_products(1, 0, lambda p: True, 1, False)
    with scope("send1"):
        send_products(1)
    with scope("sums0c"):
        sums_start(0, 2, sums_finish(0, 1))
    with scope("own1"):
        own_products(1)
    with scope("sums0d"):
        total = sums_finish(0, 2)
        norm0 = unpack(total, 0)
        curve0 = unpack(total, 1)
        square0 = unpack(total, 2)
        step0 = norm0 / curve0
        rate0 = curve0 / norm0
        norm1 = norm0 - 2.0 * step0 * curve0 + step0 * step0 * square0
        mix0 = norm1 / norm0
        resid[...] = base[...] - step0 * image[...]
        direct[...] = resid[...] + mix0 * base[...]
    with scope("take1"):
        take_products(1, image, twice)

    with scope("start2"):
        resid_image[...] = image[...] - step0 * twice[...]
        image_next[...] = resid_image[...] + mix0 * image[...]
        image[...] = image_next[...] - rate0 * resid[...]
    with scope("sums1"):
        q_now = image_next[...]
        sums_start(
            1,
            0,
            pack(
                fold(direct[...] * q_now),
                fold(resid[...] * q_now),
                fold(q_now * q_now),
                fold(resid[...] * resid_image[...]),
                fold(q_now * resid_image[...]),
            ),
        )
    with scope("start2b"):
        put_field(2, image[...], 0)
        start_field(2, 0)
        put_field(2, image[...], 1)
        start_field(2, 1)
        send_behind(2)
    with scope("diag2"):
        diag_products(2)
        w_now = image[...]
        local = fold(w_now * (own_part[...] + noise[...] * w_now))
    with scope("finish2"):
        finish_field(2, 0)
    with scope("early2"):
        early_cols(2, 0)
        early_cols(2, middle)
    with scope("finish2b"):
        finish_field(2, 1)
    with scope("sums1b"):
        sums_start(1, 1, sums_finish(1, 0))
    with scope("cols2"):
        col_products(2, 0)
        send_ahead(2)
        total = col_products(2, middle)
        finish_ahead(2)
    with scope("sums2"):
        sums_start(2, 0, pack(local + 2.0 * quadratic(2, total)))
    with scope("rows2"):
        row_products(2, middle, lambda p: True, 0, False)
    with scope("rows2b"):
        row_products(2, 0, lambda p: True, 1, False)
    with scope("send2"):
        send_products(2)
    with scope("sums2b"):
        sums_start(2, 1, sums_finish(2, 0))
    with scope("sums1c"):
        sums_start(1, 2, sums_finish(1, 1))
    with scope("own2"):
        own_products(2)
    with scope("sums2d"):
        total = sums_finish(1, 2)
        curve1 = unpack(total, 0)
        cross1 = unpack(total, 1)
        square1 = unpack(total, 2)
        inner_rr = unpack(total, 3)
        inner_qr = unpack(total, 4)
        step1 = norm1 / curve1
        norm2 = norm1 - 2.0 * step1 * cross1 + step1 * step1 * square1
        mix1 = norm2 / norm1
        keep = 1.0 - step1 * rate0
        inner_ww = unpack(sums_finish(2, 1), 0)
        inner_wr = inner_qr - rate0 * inner_rr
        inner_wq = square1 - rate0 * cross1
        curve2 = (
            step1 * step1 * inner_ww
            + keep * keep * inner_rr
            + mix1 * mix1 * curve1
            - 2.0 * keep * step1 * inner_wr
            + 2.0 * keep * mix1 * cross1
            - 2.0 * step1 * mix1 * inner_wq
        )
        step2 = norm2 / curve2
        r_now = resid[...] - step1 * image_next[...]
        d_now = r_now + mix1 * direct[...]
        sol_ref[...] = step0 * base[...] + step1 * direct[...] + step2 * d_now
        resid[...] = r_now - step2 * (keep * resid_image[...] + mix1 * image_next[...])
    with scope("take2"):
        take_products(2, image, twice)
        res_ref[...] = resid[...] + (step2 * step1) * twice[...]

    with scope("drain"):
        for k in range(ITERS):
            drain_field(k)
            drain_products(k)
            sums_drain(k)


def solution(mesh):
    tiles, subs = mesh.shape["tile"], mesh.shape["sub"]
    side = math.isqrt(tiles // 2)

    def on_device(right_side, point_order, noise_var, block_pairs, pair_blocks, diag_blocks):
        rhs, points = right_side.shape
        slots, block = pair_blocks.shape[:2]
        blk_dev = diag_blocks.shape[0]
        cfg = (tiles, subs, side, blk_dev, block, slots, rhs)
        members = 2 * subs + max(2 * side, tiles // 2)
        vec = pltpu.VMEM((rhs, points), F32)
        row = pltpu.VMEM((ITERS, blk_dev, rhs, block), BF16)
        dma = pltpu.SemaphoreType.DMA
        return pl.pallas_call(
            functools.partial(kernel, cfg),
            out_shape=(jax.ShapeDtypeStruct((rhs, points), F32),) * 2,
            in_specs=[pl.BlockSpec(memory_space=pltpu.MemorySpace.HBM)] * 6,
            out_specs=(pl.BlockSpec(memory_space=pltpu.VMEM),) * 2,
            scratch_shapes=[
                vec,
                pltpu.VMEM((1, points), jnp.int32),
                pltpu.VMEM((1, points), F32),
                pltpu.SMEM((2, slots), jnp.int32),
                pltpu.VMEM((slots, block, block), BF16),
                pltpu.VMEM((blk_dev, block, block), BF16),
                vec,
                vec,
                vec,
                vec,
                vec,
                vec,
                vec,
                vec,
                pltpu.VMEM((ITERS, (subs + 1) * blk_dev, rhs, LANES), BF16),
                pltpu.VMEM((ITERS, (subs + 1) * blk_dev, rhs, LANES), BF16),
                pltpu.VMEM((ITERS, 2, blk_dev, rhs, LANES), BF16),
                pltpu.VMEM((1 + slots, rhs, block), F32),
                pltpu.VMEM((1 + slots, rhs, block), F32),
                pltpu.VMEM((subs * blk_dev, rhs, block), F32),
                pltpu.VMEM((slots, block, block), BF16),
                pltpu.VMEM((ITERS, 3, blk_dev, rhs, block), BF16),
                pltpu.VMEM((ITERS, 3, blk_dev, rhs, block), BF16),
                row,
                row,
                pltpu.VMEM((16, LANES), jnp.int32),
                pltpu.SMEM((16, LANES), jnp.int32),
                pltpu.VMEM((ITERS, members, 1, LANES), F32),
                dma((5,)),
                dma,
                dma,
                dma((ITERS,)),
                dma((ITERS, 2, 3)),
                dma((ITERS,)),
                dma((ITERS,)),
                dma((ITERS,)),
                dma((ITERS,)),
                dma((ITERS,)),
                dma((ITERS,)),
                dma((ITERS, 3)),
                dma((ITERS, 3)),
            ],
            compiler_params=pltpu.CompilerParams(
                collective_id=0, has_side_effects=True, vmem_limit_bytes=50 << 20
            ),
            name="block_pair_solve",
        )(
            *(
                pltpu.with_memory_space_constraint(value, pltpu.MemorySpace.HBM)
                for value in (
                    right_side,
                    point_order,
                    noise_var.reshape(1, -1),
                    block_pairs.T,
                    pair_blocks,
                    diag_blocks,
                )
            )
        )

    both = ("tile", "sub")
    return jax.shard_map(
        on_device,
        mesh=mesh,
        in_specs=(
            P(None, both),
            P(both, None),
            P(both),
            P(both, None),
            P(both, None, None),
            P(both, None, None),
        ),
        out_specs=(P(None, both), P(None, both)),
        check_vma=False,
    )
```

```python
import functools
import math

import jax
import jax.numpy as jnp
from jax import lax
from jax.experimental import pallas as pl
from jax.experimental.pallas import tpu as pltpu
from jax.sharding import PartitionSpec as P

ITERS = 3
PARTS = 6
LANES = 128
F32 = jnp.float32
BF16 = jnp.bfloat16
MESH = pl.DeviceIdType.MESH


def scope(name):
    return jax.named_scope(name)


def kernel(
    cfg,
    right_hbm,
    order_hbm,
    noise_hbm,
    pairs_hbm,
    blocks_hbm,
    diag_hbm,
    sol_ref,
    res_ref,
    right,
    order,
    noise,
    pairs,
    blocks,
    diag,
    base,
    image,
    twice,
    resid,
    direct,
    image_next,
    resid_image,
    own_part,
    field_low,
    field_high,
    field_ahead,
    col_out,
    row_out,
    half_sums,
    turned,
    parts_out,
    parts_in,
    to_ahead,
    from_behind,
    table_vec,
    table,
    sums,
    in_sem,
    blocks_sem,
    table_sem,
    field_send,
    field_recv,
    ahead_send,
    ahead_recv,
    part_send,
    part_recv,
    behind_send,
    behind_recv,
    sums_send,
    sums_recv,
):
    tiles, subs, side, blk_dev, block, slots, rhs = cfg
    t = lax.axis_index("tile")
    s = lax.axis_index("sub")
    core = lax.rem(t, 2)
    above = jnp.where(s == subs - 1, 0, s + 1)
    below = jnp.where(s == 0, subs - 1, s - 1)
    across = jnp.where(s >= subs - 2, s + 2 - subs, s + 2)
    has_behind = t > 0
    has_ahead = t < tiles - 1

    fields = (field_low, field_high)
    loads = [
        pltpu.make_async_copy(right_hbm, right, in_sem.at[0]),
        pltpu.make_async_copy(order_hbm, order, in_sem.at[1]),
        pltpu.make_async_copy(pairs_hbm, pairs, in_sem.at[2]),
        pltpu.make_async_copy(noise_hbm, noise, in_sem.at[3]),
        pltpu.make_async_copy(diag_hbm, diag, in_sem.at[4]),
    ]
    step = slots // PARTS
    block_loads = [
        pltpu.make_async_copy(
            blocks_hbm.at[pl.ds(i * step, step)],
            blocks.at[pl.ds(i * step, step)],
            blocks_sem,
        )
        for i in range(PARTS)
    ]
    for copy in (*loads[:3], loads[4], *block_loads, loads[3]):
        copy.start()

    def wrap(index, count):
        return jnp.where(index >= count, index - count, index)

    group = core * subs + s
    chip_x = lax.rem(t // 2, side)
    chip_y = t // (2 * side)
    far_ahead = (core == 1) & has_ahead
    far_behind = (core == 0) & has_behind
    other_core = t + 1 - 2 * core
    column = [(t, wrap(s + j, subs)) for j in range(1, subs)] + [
        (other_core, wrap(s + j, subs)) for j in range(subs)
    ]
    along_x = [((chip_y * side + wrap(chip_x + j, side)) * 2 + core, s) for j in range(1, side)]
    along_y = [((wrap(chip_y + j, side) * side + chip_x) * 2 + core, s) for j in range(1, side)]
    plane = []
    for i in range(side):
        for j in range(side):
            if i or j:
                at = wrap(chip_y + i, side) * side + wrap(chip_x + j, side)
                plane.append((at * 2 + core, s))

    stages = (
        (group, column, 0),
        (chip_x, along_x, 2 * subs),
        (chip_y, along_y, 2 * subs + side),
    )
    last_stages = (stages[0], (t // 2, plane, 2 * subs))

    def stages_of(k):
        return last_stages if k == ITERS - 1 else stages

    barrier = pltpu.get_barrier_semaphore()

    def greet(target):
        pl.semaphore_signal(barrier, inc=1, device_id=target, device_id_type=MESH)

    @pl.when(far_ahead)
    def _():
        @pl.when(s > 0)
        def _():
            greet((t + 1, 0))

        greet((t + 1, s))

    @pl.when(far_behind)
    def _():
        @pl.when(s == 0)
        def _():
            for j in range(1, subs):
                greet((t - 1, j))

        greet((t - 1, s))

    greeted = 0
    for unused, members, also_unused in stages:
        for target in members:
            greet(target)
            greeted += 1


    chunks = right.shape[1] // LANES

    def permute(i, carry):
        for u in range(4):
            chunk = (i % (chunks // 8) * 4 + u) * 2 + i // (chunks // 8)
            at = pl.multiple_of(chunk * LANES, LANES)
            index = jnp.broadcast_to(order[:, pl.ds(at, LANES)], (rhs, LANES))
            low = lax.bitwise_and(index, LANES - 1)
            high = lax.shift_right_logical(index, 7)
            out = jnp.zeros((rhs, LANES), F32)
            for h in range(chunks):
                picked = jnp.take_along_axis(right[:, h * LANES : (h + 1) * LANES], low, axis=1)
                out = jnp.where(high == h, picked, out)
            base[:, pl.ds(at, LANES)] = out
        return carry

    def put_field(k, values, h):
        for b in range(blk_dev):
            at = b * block + h * LANES
            fields[h][k, s * blk_dev + b] = values[:, at : at + LANES].astype(BF16)

    def whole(k, q):
        return jnp.concatenate([field_low[k, q], field_high[k, q]], axis=1)

    def remote(src, dst, send, recv, target):
        return pltpu.make_async_remote_copy(
            src_ref=src,
            dst_ref=dst,
            send_sem=send,
            recv_sem=recv,
            device_id=target,
            device_id_type=MESH,
        )

    targets = (across, above, below)
    sources = (across, below, above)

    def field_copy(k, row, h, n):
        part = fields[h].at[k, pl.ds(row * blk_dev, blk_dev)]
        return remote(part, part, field_send.at[k], field_recv.at[k, h, n], (t, targets[n]))

    def ahead_copy(k, h, to):
        return remote(
            fields[h].at[k, pl.ds(0, blk_dev)],
            field_ahead.at[k, h],
            ahead_send.at[k],
            ahead_recv.at[k],
            (t - 1, to),
        )

    def ahead_waits(k):
        both = field_ahead.at[k]
        return remote(both, both, ahead_send.at[k], ahead_recv.at[k], (t, above))

    def pass_back(k, row, h):
        @pl.when((row == 0) & (core == 1))
        def _():
            ahead_copy(k, h, s).start()

    def send_behind(k):
        @pl.when((s == 0) & far_behind)
        def _():
            for h in range(2):
                for j in (2, 1, 3, 0):
                    ahead_copy(k, h, j).start()

    def start_field(k, h):
        for n in range(3):
            field_copy(k, s, h, n).start()
        pass_back(k, s, h)

    def finish_field(k, h):
        for n in (1, 2, 0):
            field_copy(k, sources[n], h, n).wait_recv()
            pass_back(k, sources[n], h)

    def finish_ahead(k):
        @pl.when(has_ahead)
        def _():
            ahead_waits(k).wait_recv()

        for h in range(2):
            for b in range(blk_dev):
                fields[h][k, subs * blk_dev + b] = field_ahead[k, h, b]

    def drain_field(k):
        sent = parts_out.at[k]
        remote(sent, sent, field_send.at[k], field_recv.at[k, 0, 0], (t, above)).wait_send()

        @pl.when(core == 1)
        def _():
            ahead_waits(k).wait_send()

        @pl.when((s == 0) & far_behind)
        def _():
            sent = field_low.at[pl.ds(0, 2), pl.ds(0, subs * blk_dev)]
            remote(sent, sent, ahead_send.at[k], ahead_recv.at[k], (t, above)).wait_send()

    def sums_start(k, stage, values):
        mine, members, offset = stages_of(k)[stage]
        sums[k, offset + mine] = values
        own = sums.at[k, offset + mine]
        for target in members:
            remote(own, own, sums_send.at[k, stage], sums_recv.at[k, stage], target).start()

    def sums_waits(k, stage):
        mine, members, offset = stages_of(k)[stage]
        others = sums.at[k, pl.ds(offset, len(members))]
        return remote(
            others, others, sums_send.at[k, stage], sums_recv.at[k, stage], (t, above)
        )

    def sums_finish(k, stage):
        mine, members, offset = stages_of(k)[stage]
        sums_waits(k, stage).wait_recv()
        total = sums[k, offset]
        for j in range(1, len(members) + 1):
            total = total + sums[k, offset + j]
        return total

    def sums_drain(k):
        for stage in range(len(stages_of(k))):
            sums_waits(k, stage).wait_send()

    def fold(values):
        parts = [values[:, i : i + LANES] for i in range(0, values.shape[1], LANES)]
        while len(parts) > 1:
            parts = [a + b for a, b in zip(parts[::2], parts[1::2])]
        return parts[0]

    spot = lax.broadcasted_iota(jnp.int32, (rhs, LANES), 1) - lax.broadcasted_iota(
        jnp.int32, (rhs, LANES), 0
    )

    def pack(*folded):
        out = jnp.zeros((rhs, LANES), F32)
        for n, values in enumerate(folded):
            column = jnp.sum(values, axis=1, keepdims=True)
            out = jnp.where(spot == n * rhs, column, out)
        return jnp.sum(out, axis=0, keepdims=True)

    def unpack(total, n):
        wide = jnp.broadcast_to(total, (rhs, LANES))
        return jnp.sum(jnp.where(spot == n * rhs, wide, 0.0), axis=1, keepdims=True)

    first = t * (subs * blk_dev)
    middle = slots // 2
    tile_blocks = subs * blk_dev

    def build_table():
        shape = (8, LANES)
        sub_id = lax.broadcasted_iota(jnp.int32, shape, 0)
        lane_id = lax.broadcasted_iota(jnp.int32, shape, 1)
        ids = sub_id * LANES + lane_id

        def add_slot(i, carry):
            found, listed, low, high = carry
            for u in range(8):
                p = i * 8 + u
                row = pairs[0, p]
                col = pairs[1, p]
                live = row >= 0
                reach = jnp.where(col - first >= tile_blocks, 1, 0)
                place = jnp.where(reach == 1, low, high)
                low = low + reach
                high = high - (1 - reach)
                apart = col - row
                kind = jnp.where(apart == 1, 0, apart - (blk_dev - 2))
                key_col = jnp.where(live, (col - first) * 4 + kind, -1)
                key_row = jnp.where(live, (row - first) * 4 + kind + 4 * LANES, -1)
                found = jnp.where((ids == key_col) | (ids == key_row), place + 1, found)
                entry = jnp.where(
                    sub_id == 0,
                    p,
                    jnp.where(
                        sub_id == 1, jnp.maximum(row - first, 0), jnp.maximum(col - first, 0)
                    ),
                )
                listed = jnp.where(lane_id == place, entry, listed)
            return found, listed, low, high

        zeros = jnp.zeros(shape, jnp.int32)
        found, listed, unused_low, unused_high = lax.fori_loop(
            0, slots // 8, add_slot, (zeros, zeros, jnp.int32(0), jnp.int32(slots - 1))
        )
        table_vec[0:8] = found
        table_vec[8:16] = listed
        move = pltpu.make_async_copy(table_vec, table, table_sem)
        move.start()
        move.wait()
        col_out[0] = jnp.zeros((rhs, block), F32)
        row_out[0] = jnp.zeros((rhs, block), F32)

    def diag_products(k):
        def body(i, carry):
            for u in range(8):
                b = i * 8 + u
                at = pl.multiple_of(b * block, block)
                own_part[:, pl.ds(at, block)] = jnp.dot(
                    whole(k, s * blk_dev + b), diag[b], preferred_element_type=F32
                )
            return carry

        lax.fori_loop(0, blk_dev // 8, body, 0)

    def listed_sum(out, line, q, kinds):
        at = q * 4
        if isinstance(q, int):
            row, lane = line + at // LANES, at % LANES
        else:
            row = line + lax.shift_right_logical(at, 7)
            lane = lax.bitwise_and(at, LANES - 1)
        parts = [out[table[row, lane + n]] for n in kinds]
        while len(parts) > 1:
            paired = [x + y for x, y in zip(parts[::2], parts[1::2])]
            parts = paired + parts[len(paired) * 2 :]
        return parts[0]

    across_rows = (((1,), (0,)), ((), ()))
    across_cols = (((1,), (1,)), ((), ()))

    def turn(p):
        turned[p] = blocks[table[8, p]].T

    def dot(left, right_block, dims):
        return lax.dot_general(left, right_block, dims, preferred_element_type=F32)

    def early_cols(k, low, also=()):
        for u in range(middle):
            p = low + u
            left = field_low[k, table[9, p]]
            col_out[1 + p] = dot(left, blocks[table[8, p], :LANES], across_rows)
            if u % 2 == 0 and u // 2 < len(also):
                turn(also[u // 2])

    def col_products(k, low):
        total = jnp.zeros((rhs, block), F32)
        for u in range(middle):
            p = low + u
            left = field_high[k, table[9, p]]
            out = col_out[1 + p] + dot(left, blocks[table[8, p], LANES:], across_rows)
            col_out[1 + p] = out
            if k == ITERS - 1 and low > 0:
                total = total + out * whole(k, table[10, p]).astype(F32)
        return total

    def early_rows(k):
        for p in range(middle, slots):
            left = field_low[k, table[10, p]]
            row_out[1 + p] = dot(left, turned[p, :LANES], across_rows)

    def row_products(k, low, is_turned, line, is_early, also=()):
        share = tile_blocks // 2
        for u in range(middle):
            p = low + u
            if is_early:
                left = field_high[k, table[10, p]]
                out = row_out[1 + p] + dot(left, turned[p, LANES:], across_rows)
            elif is_turned(p):
                out = dot(whole(k, table[10, p]), turned[p], across_rows)
            else:
                out = dot(whole(k, table[10, p]), blocks[table[8, p]], across_cols)
            row_out[1 + p] = out
            if u < share:
                q = line * share + u
                half_sums[q] = listed_sum(col_out, 0, q, range(4))
            if u % 2 == 0 and u // 2 < len(also):
                turn(also[u // 2])

    def quadratic(k, total):
        def body(i, total):
            for u in range(8):
                p = i * 8 + u
                total = total + col_out[1 + p] * whole(k, table[10, p]).astype(F32)
            return total

        return fold(lax.fori_loop(0, middle // 8, body, total))

    def partial_sum(row, b):
        q = row * blk_dev + b
        return half_sums[q] + listed_sum(row_out, 4, q, range(4))

    def part_copy(k, n):
        return remote(
            parts_out.at[k, n], parts_in.at[k, n], part_send.at[k], part_recv.at[k], (t, targets[n])
        )

    def part_waits(k):
        return remote(
            parts_out.at[k], parts_in.at[k], part_send.at[k], part_recv.at[k], (t, above)
        )

    def behind_copy(k):
        return remote(
            to_ahead.at[k],
            from_behind.at[k],
            behind_send.at[k],
            behind_recv.at[k],
            (t + 1, s),
        )

    def send_ahead(k):
        @pl.when(has_ahead)
        def _():
            def body(i, carry):
                for u in range(8):
                    b = i * 8 + u
                    q = subs * blk_dev + b
                    to_ahead[k, b] = listed_sum(col_out, 0, q, (1, 2, 3)).astype(BF16)
                return carry

            lax.fori_loop(0, blk_dev // 8, body, 0)
            behind_copy(k).start()

    def send_products(k):
        @pl.when(has_behind)
        def _():
            behind_copy(k).wait_recv()

        for b in range(blk_dev):
            half_sums[b] = half_sums[b] + from_behind[k, b].astype(F32)

        for n in range(3):

            def body(i, carry):
                for u in range(8):
                    b = i * 8 + u
                    parts_out[k, n, b] = partial_sum(targets[n], b).astype(BF16)
                return carry

            lax.fori_loop(0, blk_dev // 8, body, 0)
            part_copy(k, n).start()

    def own_products(k):
        def body(i, carry):
            for u in range(4):
                b = i * 4 + u
                at = pl.ds(pl.multiple_of(b * block, block), block)
                own_part[:, at] = own_part[:, at] + partial_sum(s, b)
            return carry

        lax.fori_loop(0, blk_dev // 4, body, 0)

    def take_products(k, vector, out):
        part_waits(k).wait_recv()
        for b in range(blk_dev):
            at = slice(b * block, (b + 1) * block)
            total = parts_in[k, 0, b].astype(F32) + parts_in[k, 1, b].astype(F32)
            total = total + parts_in[k, 2, b].astype(F32)
            out[:, at] = total + (own_part[:, at] + noise[:, at] * vector[:, at])

    def drain_products(k):
        part_waits(k).wait_send()

        @pl.when(has_ahead)
        def _():
            behind_copy(k).wait_send()


    loads[0].wait()
    loads[1].wait()
    with scope("permute0"):
        lax.fori_loop(0, chunks // 8, permute, 0)
        put_field(0, base[...], 0)
    with scope("barrier"):
        pl.semaphore_wait(barrier, greeted
            + jnp.where(far_ahead | far_behind, 1, 0)
            + jnp.where(far_ahead & (s > 0), 1, 0)
            + jnp.where(far_behind & (s == 0), subs - 1, 0))
    start_field(0, 0)
    with scope("permute1"):
        lax.fori_loop(chunks // 8, chunks // 4, permute, 0)
        put_field(0, base[...], 1)
    start_field(0, 1)
    send_behind(0)

    @pl.when(jnp.logical_not(has_ahead))
    def _():
        for k in range(ITERS):
            field_ahead[k] = jnp.zeros((2, blk_dev, rhs, LANES), BF16)

    @pl.when(jnp.logical_not(has_behind))
    def _():
        for k in range(ITERS):
            from_behind[k] = jnp.zeros((blk_dev, rhs, block), BF16)

    loads[2].wait()
    with scope("table"):
        build_table()
    loads[4].wait()
    with scope("diag0"):
        diag_products(0)
    pltpu.make_async_copy(blocks_hbm, blocks, blocks_sem).wait()
    with scope("finish0"):
        finish_field(0, 0)
    with scope("early0"):
        quarter = middle // 2
        early_cols(0, 0, range(middle, middle + quarter))
        early_cols(0, middle, range(middle + quarter, slots))
        early_rows(0)
    with scope("finish0b"):
        finish_field(0, 1)
    with scope("cols0"):
        col_products(0, 0)
        send_ahead(0)
        col_products(0, middle)
    with scope("rows0"):
        row_products(0, middle, lambda p: True, 0, True, range(quarter))
        finish_ahead(0)
        row_products(0, 0, lambda p: p < quarter, 1, False, range(quarter, middle))
    with scope("send0"):
        send_products(0)
    with scope("own0"):
        own_products(0)
    loads[3].wait()
    with scope("take0"):
        take_products(0, base, image)

    with scope("sums0"):
        b_now = base[...]
        q_now = image[...]
        sums_start(0, 0, pack(fold(b_now * b_now), fold(b_now * q_now), fold(q_now * q_now)))
    with scope("start1"):
        put_field(1, image[...], 0)
        start_field(1, 0)
        put_field(1, image[...], 1)
        start_field(1, 1)
        send_behind(1)
    with scope("diag1"):
        diag_products(1)
    with scope("finish1"):
        finish_field(1, 0)
    with scope("early1"):
        early_cols(1, 0)
        early_cols(1, middle)
        early_rows(1)
    with scope("finish1b"):
        finish_field(1, 1)
    with scope("sums0b"):
        sums_start(0, 1, sums_finish(0, 0))
    with scope("cols1"):
        col_products(1, 0)
        send_ahead(1)
        col_products(1, middle)
    with scope("rows1"):
        row_products(1, middle, lambda p: True, 0, True)
    with scope("rows1b"):
        finish_ahead(1)
        row_products(1, 0, lambda p: True, 1, False)
    with scope("send1"):
        send_products(1)
    with scope("sums0c"):
        sums_start(0, 2, sums_finish(0, 1))
    with scope("own1"):
        own_products(1)
    with scope("sums0d"):
        total = sums_finish(0, 2)
        norm0 = unpack(total, 0)
        curve0 = unpack(total, 1)
        square0 = unpack(total, 2)
        step0 = norm0 / curve0
        rate0 = curve0 / norm0
        norm1 = norm0 - 2.0 * step0 * curve0 + step0 * step0 * square0
        mix0 = norm1 / norm0
        resid[...] = base[...] - step0 * image[...]
        direct[...] = resid[...] + mix0 * base[...]
    with scope("take1"):
        take_products(1, image, twice)

    with scope("start2"):
        resid_image[...] = image[...] - step0 * twice[...]
        image_next[...] = resid_image[...] + mix0 * image[...]
        image[...] = image_next[...] - rate0 * resid[...]
    with scope("sums1"):
        q_now = image_next[...]
        sums_start(
            1,
            0,
            pack(
                fold(direct[...] * q_now),
                fold(resid[...] * q_now),
                fold(q_now * q_now),
                fold(resid[...] * resid_image[...]),
                fold(q_now * resid_image[...]),
            ),
        )
    with scope("start2b"):
        put_field(2, image[...], 0)
        start_field(2, 0)
        put_field(2, image[...], 1)
        start_field(2, 1)
        send_behind(2)
    with scope("diag2"):
        diag_products(2)
        w_now = image[...]
        local = fold(w_now * (own_part[...] + noise[...] * w_now))
    with scope("finish2"):
        finish_field(2, 0)
    with scope("early2"):
        early_cols(2, 0)
        early_cols(2, middle)
    with scope("finish2b"):
        finish_field(2, 1)
    with scope("sums1b"):
        sums_start(1, 1, sums_finish(1, 0))
    with scope("cols2"):
        col_products(2, 0)
        send_ahead(2)
        total = col_products(2, middle)
        finish_ahead(2)
    with scope("sums2"):
        sums_start(2, 0, pack(local + 2.0 * quadratic(2, total)))
    with scope("rows2"):
        row_products(2, middle, lambda p: True, 0, False)
    with scope("rows2b"):
        row_products(2, 0, lambda p: True, 1, False)
    with scope("send2"):
        send_products(2)
    with scope("sums2b"):
        sums_start(2, 1, sums_finish(2, 0))
    with scope("sums1c"):
        sums_start(1, 2, sums_finish(1, 1))
    with scope("own2"):
        own_products(2)
    with scope("sums2d"):
        total = sums_finish(1, 2)
        curve1 = unpack(total, 0)
        cross1 = unpack(total, 1)
        square1 = unpack(total, 2)
        inner_rr = unpack(total, 3)
        inner_qr = unpack(total, 4)
        step1 = norm1 / curve1
        norm2 = norm1 - 2.0 * step1 * cross1 + step1 * step1 * square1
        mix1 = norm2 / norm1
        keep = 1.0 - step1 * rate0
        inner_ww = unpack(sums_finish(2, 1), 0)
        inner_wr = inner_qr - rate0 * inner_rr
        inner_wq = square1 - rate0 * cross1
        curve2 = (
            step1 * step1 * inner_ww
            + keep * keep * inner_rr
            + mix1 * mix1 * curve1
            - 2.0 * keep * step1 * inner_wr
            + 2.0 * keep * mix1 * cross1
            - 2.0 * step1 * mix1 * inner_wq
        )
        step2 = norm2 / curve2
        r_now = resid[...] - step1 * image_next[...]
        d_now = r_now + mix1 * direct[...]
        sol_ref[...] = step0 * base[...] + step1 * direct[...] + step2 * d_now
        resid[...] = r_now - step2 * (keep * resid_image[...] + mix1 * image_next[...])
    with scope("take2"):
        take_products(2, image, twice)
        res_ref[...] = resid[...] + (step2 * step1) * twice[...]

    with scope("drain"):
        for k in range(ITERS):
            drain_field(k)
            drain_products(k)
            sums_drain(k)


def solution(mesh):
    tiles, subs = mesh.shape["tile"], mesh.shape["sub"]
    side = math.isqrt(tiles // 2)

    def on_device(right_side, point_order, noise_var, block_pairs, pair_blocks, diag_blocks):
        rhs, points = right_side.shape
        slots, block = pair_blocks.shape[:2]
        blk_dev = diag_blocks.shape[0]
        cfg = (tiles, subs, side, blk_dev, block, slots, rhs)
        members = 2 * subs + max(2 * side, tiles // 2)
        vec = pltpu.VMEM((rhs, points), F32)
        row = pltpu.VMEM((ITERS, blk_dev, rhs, block), BF16)
        dma = pltpu.SemaphoreType.DMA
        return pl.pallas_call(
            functools.partial(kernel, cfg),
            out_shape=(jax.ShapeDtypeStruct((rhs, points), F32),) * 2,
            in_specs=[pl.BlockSpec(memory_space=pltpu.MemorySpace.HBM)] * 6,
            out_specs=(pl.BlockSpec(memory_space=pltpu.VMEM),) * 2,
            scratch_shapes=[
                vec,
                pltpu.VMEM((1, points), jnp.int32),
                pltpu.VMEM((1, points), F32),
                pltpu.SMEM((2, slots), jnp.int32),
                pltpu.VMEM((slots, block, block), BF16),
                pltpu.VMEM((blk_dev, block, block), BF16),
                vec,
                vec,
                vec,
                vec,
                vec,
                vec,
                vec,
                vec,
                pltpu.VMEM((ITERS, (subs + 1) * blk_dev, rhs, LANES), BF16),
                pltpu.VMEM((ITERS, (subs + 1) * blk_dev, rhs, LANES), BF16),
                pltpu.VMEM((ITERS, 2, blk_dev, rhs, LANES), BF16),
                pltpu.VMEM((1 + slots, rhs, block), F32),
                pltpu.VMEM((1 + slots, rhs, block), F32),
                pltpu.VMEM((subs * blk_dev, rhs, block), F32),
                pltpu.VMEM((slots, block, block), BF16),
                pltpu.VMEM((ITERS, 3, blk_dev, rhs, block), BF16),
                pltpu.VMEM((ITERS, 3, blk_dev, rhs, block), BF16),
                row,
                row,
                pltpu.VMEM((16, LANES), jnp.int32),
                pltpu.SMEM((16, LANES), jnp.int32),
                pltpu.VMEM((ITERS, members, 1, LANES), F32),
                dma((5,)),
                dma,
                dma,
                dma((ITERS,)),
                dma((ITERS, 2, 3)),
                dma((ITERS,)),
                dma((ITERS,)),
                dma((ITERS,)),
                dma((ITERS,)),
                dma((ITERS,)),
                dma((ITERS,)),
                dma((ITERS, 3)),
                dma((ITERS, 3)),
            ],
            compiler_params=pltpu.CompilerParams(
                collective_id=0, has_side_effects=True, vmem_limit_bytes=50 << 20
            ),
            name="block_pair_solve",
        )(
            *(
                pltpu.with_memory_space_constraint(value, pltpu.MemorySpace.HBM)
                for value in (
                    right_side,
                    point_order,
                    noise_var.reshape(1, -1),
                    block_pairs.T,
                    pair_blocks,
                    diag_blocks,
                )
            )
        )

    both = ("tile", "sub")
    return jax.shard_map(
        on_device,
        mesh=mesh,
        in_specs=(
            P(None, both),
            P(both, None),
            P(both),
            P(both, None),
            P(both, None, None),
            P(both, None, None),
        ),
        out_specs=(P(None, both), P(None, both)),
        check_vma=False,
    )
```
